768 devices in a mesh: ctx: 384 (over z, y, x), head: 2 (over core).
Axes of the slice: x: 4, y: 8, z: 12, core: 2. Of those that a mesh axis runs over, the one named last changes fastest.
Arguments:
- queries: bfloat16 [98304, 4, 256], P('ctx', 'head'), may hold values from -6 to 6
- token_keys: bfloat16 [98304, 4, 256], P('ctx', 'head'), may hold values from -6 to 6
- token_values: bfloat16 [98304, 4, 256], P('ctx', 'head'), may hold values from -6 to 6
- step_rates: float32 [98304, 4], P('ctx', 'head'), may hold values from 0.1 to 1
- counts: int32 [384], replicated, may hold values from 64 to 256, as said below
- fast_weights: float32 [4, 3, 256, 256], P('head'), may hold values from -0.375 to 0.375
- out_weight: bfloat16 [1024, 4096], P('head'), may hold values from -0.1875 to 0.1875
Outputs:
- layer_output: bfloat16 [98304, 4096], P('ctx', 'head')
The draws below stay inside these ranges and needn't reach their ends.
Inputs may be any that keep to these rules, and one draw needn't show every extreme that they name: counts[i] tokens at the start of block i are valid, the rest are padding; some block is full and some holds exactly 64.
All inputs are finite; a program needn't handle non-finite values.
Results may differ from the reference program's by a relative error of at most 0.012.
The reference program's roundings to bfloat16 on the way count: a program that leaves them out, or rounds other values in their place, can miss the bound.
Values may be sent and summed in bfloat16 or wider, within the bound.
No kernel may reach another device: no remote copies, remote signals or barrier semaphores. Data moves between devices by JAX's collectives and lax.ppermute only.
A program may use at most 32 MiB of HBM per device.

```python
import math
import jax
import jax.numpy as jnp
from jax import lax

HS = 256
DM = 4096
TOK_DEV = 256
WINDOW = 512
HEADS = 4
BLOCKS = 384
TOKENS = 98304


def draw_queries(key, part):
    result = jnp.clip(1.4 * jax.random.normal(jax.random.fold_in(key, 1), (TOKENS, HEADS, HS), jnp.float32), -6.0, 6.0)
    return result.astype(jnp.bfloat16)


def draw_token_keys(key, part):
    result = jnp.clip(1.4 * jax.random.normal(jax.random.fold_in(key, 2), (TOKENS, HEADS, HS), jnp.float32), -6.0, 6.0)
    return result.astype(jnp.bfloat16)


def draw_counts(key, part):
    drawn = jax.random.randint(jax.random.fold_in(key, 3), (BLOCKS,), TOK_DEV // 4, TOK_DEV + 1)
    fullest = jax.random.randint(jax.random.fold_in(key, 5), (), 0, BLOCKS)
    offset = jax.random.randint(jax.random.fold_in(key, 9), (), 1, BLOCKS)
    smallest = (fullest + offset) % BLOCKS
    drawn = drawn.at[fullest].set(TOK_DEV)
    drawn = drawn.at[smallest].set(TOK_DEV // 4)
    return drawn.astype(jnp.int32)


def shard_levels(own_key, dims, shards, low, high):
    loudness, own = 1.0, jax.random.fold_in(own_key, 6)
    for dim, parts in shards:
        draws = jnp.exp(jax.random.uniform(jax.random.fold_in(own, dim), (parts,), jnp.float32, low / len(shards), high / len(shards)))
        loudness = loudness * jnp.repeat(draws, dims[dim] // parts).reshape([-1 if axis == dim else 1 for axis in range(len(dims))])
    return loudness


def normal_values(rng, dims, spread, bound, split=(), kind=jnp.bfloat16):
    values = jax.random.normal(rng, dims, jnp.float32) * spread
    if len(split) > 0:
        values = shard_levels(rng, dims, split, -0.22, 0.18) * values
    return jnp.clip(values, min=-bound, max=bound).astype(kind)


def setup_inputs(seed: int = 0) -> dict:
    streams_of = jax.random.split(jax.random.key(seed), 8)
    queries = draw_queries(jax.random.fold_in(streams_of[7], 71), 0)
    token_keys = draw_token_keys(jax.random.fold_in(streams_of[7], 71), 0)
    token_values = normal_values(streams_of[2], (TOKENS, HEADS, HS), 1.0, 6.0, ((0, 384), (1, 2)))
    step_rates = jnp.clip(jnp.exp(math.log(1.0) - 2.3025851 * jax.random.uniform(streams_of[3], (TOKENS, HEADS), jnp.float32) ** shard_levels(streams_of[3], (TOKENS, HEADS), ((0, 384), (1, 2)), -0.2, 0.2)), 0.1, 1.0)
    counts = draw_counts(jax.random.fold_in(streams_of[7], 71), 0)
    fast_weights = normal_values(streams_of[5], (HEADS, 3, HS, HS), HS ** -0.5, 0.375, ((0, 2),), jnp.float32)
    out_weight = normal_values(streams_of[6], (HEADS * HS, DM), (HEADS * HS) ** -0.5, 0.1875, ((0, 2),))
    return {"queries": queries, "token_keys": token_keys, "token_values": token_values, "step_rates": step_rates, "counts": counts, "fast_weights": fast_weights, "out_weight": out_weight}


def rounded(values_in):
    return lax.optimization_barrier(values_in.astype(jnp.bfloat16)).astype(jnp.float32)

def silu_slope(pre_value):
    sigmoid_value = jax.nn.sigmoid(pre_value)
    return sigmoid_value * (1.0 + pre_value * (1.0 - sigmoid_value))

def block_gradient(key_block, scaled_block, weights_wide):
    keys_wide = key_block.astype(jnp.float32)
    gate_pre = jnp.einsum('thi,hci->thc', keys_wide, weights_wide[:, 0])
    up_pre = jnp.einsum('thi,hci->thc', keys_wide, weights_wide[:, 1])
    gate_act = jax.nn.silu(gate_pre)
    hidden = rounded(gate_act * up_pre)
    grad_down = -jnp.einsum('thd,thc->hdc', scaled_block, hidden)
    back_hidden = -jnp.einsum('thd,hdc->thc', scaled_block, weights_wide[:, 2])
    grad_gate = rounded(back_hidden * up_pre * silu_slope(gate_pre))
    grad_up = rounded(back_hidden * gate_act)
    first_grad = jnp.einsum('thc,thi->hci', grad_gate, keys_wide)
    second_grad = jnp.einsum('thc,thi->hci', grad_up, keys_wide)
    return jnp.stack([first_grad, second_grad, grad_down], axis=1)

def reference(queries, token_keys, token_values, step_rates, counts, fast_weights, out_weight):
    positions = jnp.arange(TOKENS, dtype=jnp.int32)
    valid_rows = (positions % TOK_DEV < counts[positions // TOK_DEV]).astype(jnp.float32)
    weights_wide = rounded(fast_weights)

    def add_block(total, block_index):
        start = (block_index * TOK_DEV).astype(jnp.int32)
        key_block = lax.dynamic_slice_in_dim(token_keys, start, TOK_DEV, 0)
        value_block = lax.dynamic_slice_in_dim(token_values, start, TOK_DEV, 0).astype(jnp.float32)
        rate_block = lax.dynamic_slice_in_dim(step_rates, start, TOK_DEV, 0)
        valid_block = lax.dynamic_slice_in_dim(valid_rows, start, TOK_DEV, 0)
        scaled_block = rounded((rate_block * valid_block[:, None])[:, :, None] * value_block)
        return (total + block_gradient(key_block, scaled_block, weights_wide), None)
    gradient, _ = lax.scan(add_block, jnp.zeros((HEADS, 3, HS, HS), jnp.float32), jnp.arange(BLOCKS, dtype=jnp.int32))
    updated = fast_weights - gradient / math.sqrt(TOKENS)
    old_norm = jnp.sqrt(lax.optimization_barrier(jnp.sum(fast_weights * fast_weights, axis=-1, keepdims=True)))
    new_weights = rounded(updated * old_norm / jnp.sqrt(lax.optimization_barrier(jnp.sum(updated * updated, axis=-1, keepdims=True)) + 1e-06))
    pad_keys = jnp.concatenate([jnp.zeros((WINDOW, HEADS, HS), jnp.bfloat16), token_keys], 0)
    pad_values = jnp.concatenate([jnp.zeros((WINDOW, HEADS, HS), jnp.bfloat16), token_values], 0)
    pad_valid = jnp.concatenate([jnp.zeros((WINDOW,), jnp.float32), valid_rows], 0)
    distance = WINDOW + jnp.arange(TOK_DEV, dtype=jnp.int32)[:, None] - jnp.arange(WINDOW + TOK_DEV, dtype=jnp.int32)[None, :]

    def one_block(block_index):
        start = (block_index * TOK_DEV).astype(jnp.int32)
        query_block = lax.dynamic_slice_in_dim(queries, start, TOK_DEV, 0).astype(jnp.float32)
        query_valid = lax.dynamic_slice_in_dim(valid_rows, start, TOK_DEV, 0)
        seen_keys = lax.dynamic_slice_in_dim(pad_keys, start, WINDOW + TOK_DEV, 0).astype(jnp.float32)
        seen_values = lax.dynamic_slice_in_dim(pad_values, start, WINDOW + TOK_DEV, 0).astype(jnp.float32)
        seen_valid = lax.dynamic_slice_in_dim(pad_valid, start, WINDOW + TOK_DEV, 0)
        query_gate = jnp.einsum('thi,hci->thc', query_block, new_weights[:, 0])
        query_up = jnp.einsum('thi,hci->thc', query_block, new_weights[:, 1])
        query_hidden = rounded(jax.nn.silu(query_gate) * query_up)
        ttt_out = jnp.einsum('thc,hdc->thd', query_hidden, new_weights[:, 2])
        scores = jnp.einsum('thi,shi->hts', query_block, seen_keys) / math.sqrt(HS)
        allowed = (distance >= 0) & (distance < WINDOW) & (seen_valid[None, :] > 0.5)
        scores = jnp.where(allowed[None], scores, -1e+30)
        top_score = lax.optimization_barrier(jnp.max(scores, axis=-1, keepdims=True))
        expo = jnp.exp(scores - top_score)
        attention = rounded(expo / lax.optimization_barrier(jnp.sum(expo, axis=-1, keepdims=True)))
        window_out = jnp.einsum('hts,shd->thd', attention, seen_values)
        features = ((ttt_out + window_out) * query_valid[:, None, None]).astype(jnp.bfloat16)
        features = features.reshape(TOK_DEV, HEADS * HS)
        return jnp.dot(features, out_weight, preferred_element_type=jnp.float32).astype(jnp.bfloat16)
    outputs = lax.map(one_block, jnp.arange(BLOCKS, dtype=jnp.int32))
    return outputs.reshape(TOKENS, DM)
```

```python
import math

import jax
import jax.numpy as jnp
from jax import lax
from jax.sharding import Mesh, PartitionSpec as P

SPAN = 2
RING = 4


def passed_along(value, axes, steps):
    count = lax.axis_size(axes)
    return lax.ppermute(value, axes, [(source, source + steps) for source in range(count - steps)])


def beside(value):
    return lax.ppermute(value, "z", [(place, place ^ 1) for place in range(RING)])


def across(value):
    return lax.ppermute(value, "z", [(place, RING - 1 - place) for place in range(RING)])


def pick(value, place):
    return lax.dynamic_index_in_dim(value, place, 0, keepdims=False)


def joined(mine, theirs, place):
    ahead = jnp.where(place == 0, mine, theirs)
    behind = jnp.where(place == 0, theirs, mine)
    return jnp.stack([ahead, behind], 0)


def silu_slope(pre_value):
    sigmoid_value = jax.nn.sigmoid(pre_value)
    return sigmoid_value * (1.0 + pre_value * (1.0 - sigmoid_value))


def refresh(old_rows, gradient_rows, token_total):
    updated = old_rows - gradient_rows / math.sqrt(token_total)
    old_norm = jnp.sqrt(jnp.sum(old_rows * old_rows, axis=-1, keepdims=True))
    fresh = (
        updated * old_norm / jnp.sqrt(jnp.sum(updated * updated, axis=-1, keepdims=True) + 1e-06)
    )
    return fresh.astype(jnp.bfloat16)


def local_gradient(token_keys, token_values, step_rates, valid_rows, fast_weights):
    weights_low = fast_weights.astype(jnp.bfloat16)
    gate_pre = jnp.einsum(
        "thi,hci->thc", token_keys, weights_low[:, 0], preferred_element_type=jnp.float32
    )
    up_pre = jnp.einsum(
        "thi,hci->thc", token_keys, weights_low[:, 1], preferred_element_type=jnp.float32
    )
    gate_act = jax.nn.silu(gate_pre)
    hidden = (gate_act * up_pre).astype(jnp.bfloat16)
    scaled = (
        (step_rates * valid_rows[:, None])[:, :, None] * token_values.astype(jnp.float32)
    ).astype(jnp.bfloat16)
    grad_down = -jnp.einsum("thd,thc->hdc", scaled, hidden, preferred_element_type=jnp.float32)
    back_hidden = -jnp.einsum(
        "thd,hdc->thc", scaled, weights_low[:, 2], preferred_element_type=jnp.float32
    )
    grad_gate = (back_hidden * up_pre * silu_slope(gate_pre)).astype(jnp.bfloat16)
    grad_up = (back_hidden * gate_act).astype(jnp.bfloat16)
    first_grad = jnp.einsum(
        "thc,thi->hci", grad_gate, token_keys, preferred_element_type=jnp.float32
    )
    second_grad = jnp.einsum(
        "thc,thi->hci", grad_up, token_keys, preferred_element_type=jnp.float32
    )
    return jnp.stack([first_grad, second_grad, grad_down], axis=1)


def summed_rows(local_grad, low_bit, high_bit):
    width = local_grad.shape[-1]
    sent = local_grad.astype(jnp.bfloat16).reshape(2, 2, 2, -1, width)
    first, second = sent[0], jnp.swapaxes(sent[1], 0, 1)
    with jax.named_scope("scatter_one"):
        first_in = beside(pick(first, 1 - low_bit))
        second_in = across(pick(second, 1 - high_bit))
    first = pick(first, low_bit).astype(jnp.float32) + first_in.astype(jnp.float32)
    second = pick(second, high_bit).astype(jnp.float32) + second_in.astype(jnp.float32)
    first, second = first.astype(jnp.bfloat16), second.astype(jnp.bfloat16)
    with jax.named_scope("scatter_two"):
        first_in = across(pick(first, 1 - high_bit))
        second_in = beside(pick(second, 1 - low_bit))
    first = pick(first, high_bit).astype(jnp.float32) + first_in.astype(jnp.float32)
    second = pick(second, low_bit).astype(jnp.float32) + second_in.astype(jnp.float32)
    rows = jnp.concatenate([first, second], 0).astype(jnp.bfloat16)
    peers = lax.axis_size("p")
    with jax.named_scope("scatter_rest"):
        blocks = lax.all_to_all(rows.reshape(peers, -1, width), "p", 0, 0, tiled=True)
    return jnp.sum(blocks.astype(jnp.float32), axis=0)


def gathered_rows(rows, low_bit, high_bit):
    width = rows.shape[-1]
    peers = lax.axis_size("p")
    with jax.named_scope("gather_rest"):
        copies = jnp.broadcast_to(rows[None], (peers, *rows.shape))
        held = lax.all_to_all(copies, "p", 0, 0, tiled=True)
    held = held.reshape(2, -1, width)
    first, second = held[0], held[1]
    with jax.named_scope("gather_one"):
        first_in = across(first)
        second_in = beside(second)
    first = joined(first, first_in, high_bit)
    second = joined(second, second_in, low_bit)
    with jax.named_scope("gather_two"):
        first_in = beside(first)
        second_in = across(second)
    first = joined(first, first_in, low_bit)
    second = jnp.swapaxes(joined(second, second_in, high_bit), 0, 1)
    return jnp.stack([first, second], 0).reshape(-1, width)


def shards(queries, token_keys, token_values, step_rates, counts, fast_weights, out_weight):
    tok_rows, head_local, head_width = queries.shape
    device_count = lax.axis_size(("z", "p"))
    device_place = lax.axis_index(("z", "p"))
    ring_place, plane_place = lax.axis_index("z"), lax.axis_index("p")
    low_bit = ((ring_place + 1) // 2) % 2
    high_bit = ring_place // 2
    with jax.named_scope("halo"):
        moved = [
            passed_along(jnp.concatenate([token_keys, token_values], 1), ("z", "p"), back_step)
            for back_step in range(SPAN, 0, -1)
        ]
    head_place = lax.axis_index("head")
    out_parts = out_weight.reshape(out_weight.shape[0], 2, -1)
    with jax.named_scope("weight_swap"):
        out_other = lax.ppermute(
            lax.dynamic_index_in_dim(out_parts, 1 - head_place, 1, keepdims=False),
            "head",
            [(0, 1), (1, 0)],
        )
    out_own = lax.dynamic_index_in_dim(out_parts, head_place, 1, keepdims=False)
    positions = jnp.arange(tok_rows, dtype=jnp.int32)
    own_count = lax.dynamic_index_in_dim(counts, device_place, 0, keepdims=False)
    valid_rows = (positions < own_count).astype(jnp.float32)
    local_grad = local_gradient(token_keys, token_values, step_rates, valid_rows, fast_weights)
    local_grad = local_grad.reshape(-1, head_width)
    old_flat = fast_weights.reshape(-1, head_width)
    token_total = tok_rows * device_count
    grad_rows = summed_rows(local_grad, low_bit, high_bit)
    quarter = old_flat.shape[0] // 8
    own_rows = grad_rows.shape[0]
    half_place = plane_place * own_rows
    color = half_place // quarter
    start = color * 4 * quarter + low_bit * 2 * quarter + high_bit * quarter
    start = start + half_place - color * quarter
    old_rows = lax.dynamic_slice_in_dim(old_flat, start, own_rows, 0)
    new_rows = refresh(old_rows, grad_rows, token_total)
    new_flat = gathered_rows(new_rows, low_bit, high_bit)
    new_weights = new_flat.reshape(head_local, 3, head_width, head_width)
    query_gate = jnp.einsum(
        "thi,hci->thc", queries, new_weights[:, 0], preferred_element_type=jnp.float32
    )
    query_up = jnp.einsum(
        "thi,hci->thc", queries, new_weights[:, 1], preferred_element_type=jnp.float32
    )
    query_hidden = (jax.nn.silu(query_gate) * query_up).astype(jnp.bfloat16)
    ttt_out = jnp.einsum(
        "thc,hdc->thd", query_hidden, new_weights[:, 2], preferred_element_type=jnp.float32
    )
    valid_parts = []
    for back_step in range(SPAN, 0, -1):
        source = device_place - back_step
        source_count = lax.dynamic_index_in_dim(counts, jnp.maximum(source, 0), 0, keepdims=False)
        valid_parts.append((positions < source_count) & (source >= 0))
    valid_parts.append(positions < own_count)
    seen_keys = jnp.concatenate([part[:, :head_local] for part in moved] + [token_keys], 0)
    seen_values = jnp.concatenate([part[:, head_local:] for part in moved] + [token_values], 0)
    seen_valid = jnp.concatenate(valid_parts, 0)
    window_len = SPAN * tok_rows
    distance = (
        window_len
        + positions[:, None]
        - jnp.arange(window_len + tok_rows, dtype=jnp.int32)[None, :]
    )
    scores = jnp.einsum(
        "thi,shi->hts", queries, seen_keys, preferred_element_type=jnp.float32
    ) / math.sqrt(head_width)
    allowed = (distance >= 0) & (distance < window_len) & seen_valid[None, :]
    scores = jnp.where(allowed[None], scores, -1e30)
    top_score = jnp.max(scores, axis=-1, keepdims=True)
    expo = jnp.exp(scores - top_score)
    attention = (expo / jnp.sum(expo, axis=-1, keepdims=True)).astype(jnp.bfloat16)
    window_out = jnp.einsum(
        "hts,shd->thd", attention, seen_values, preferred_element_type=jnp.float32
    )
    features = ((ttt_out + window_out) * valid_rows[:, None, None]).astype(jnp.bfloat16)
    features = features.reshape(tok_rows, head_local * head_width)
    with jax.named_scope("feature_swap"):
        other = lax.ppermute(features, "head", [(0, 1), (1, 0)])
    result = jnp.dot(features, out_own, preferred_element_type=jnp.float32) + jnp.dot(
        other, out_other, preferred_element_type=jnp.float32
    )
    return result.astype(jnp.bfloat16)


def solution(mesh):
    fine = Mesh(mesh.devices.reshape(RING, -1, 2), ("z", "p", "head"))
    ctx = ("z", "p")
    in_specs = (
        P(ctx, "head", None),
        P(ctx, "head", None),
        P(ctx, "head", None),
        P(ctx, "head"),
        P(),
        P("head", None, None, None),
        P("head", None),
    )
    return jax.shard_map(
        shards, mesh=fine, in_specs=in_specs, out_specs=P(ctx, "head"), check_vma=False
    )
```

```python
import math

import jax
import jax.numpy as jnp
from jax import lax
from jax.experimental import pallas as pl
from jax.experimental.pallas import tpu as pltpu
from jax.sharding import Mesh, PartitionSpec as P


RING = 4
CTX = ("z", "p")
VMEM = pl.BlockSpec(memory_space=pltpu.VMEM)
SMEM = pl.BlockSpec(memory_space=pltpu.SMEM)
LOWEST = -1e30
VMEM_BYTES = 24 << 20


def passed_along(value, steps):
    count = lax.axis_size(CTX)
    return lax.ppermute(value, CTX, [(source, source + steps) for source in range(count - steps)])


def product(left, right, left_dim, right_dim):
    return lax.dot_general(
        left,
        right,
        (((left_dim,), (right_dim,)), ((), ())),
        preferred_element_type=jnp.float32,
    )


def gradient_kernel(count_ref, keys_ref, values_ref, rates_ref, weights_ref, grad_ref):
    tokens, heads, width = keys_ref.shape
    valid = lax.broadcasted_iota(jnp.int32, (tokens, 1), 0) < count_ref[0]
    for head in range(heads):
        keys = keys_ref[:, head, :]
        values = values_ref[:, head, :].astype(jnp.float32)
        rates = jnp.where(valid, rates_ref[:, head : head + 1], 0.0)
        scaled = (rates * values).astype(jnp.bfloat16)
        gate_weight = weights_ref[head, 0].astype(jnp.bfloat16)
        up_weight = weights_ref[head, 1].astype(jnp.bfloat16)
        down_weight = weights_ref[head, 2].astype(jnp.bfloat16)
        gate_pre = product(keys, gate_weight, 1, 1)
        up_pre = product(keys, up_weight, 1, 1)
        back = -product(scaled, down_weight, 1, 0)
        sigmoid = jax.nn.sigmoid(gate_pre)
        gate_act = gate_pre * sigmoid
        hidden = (gate_act * up_pre).astype(jnp.bfloat16)
        slope = sigmoid * (1.0 + gate_pre * (1.0 - sigmoid))
        grad_gate = (back * up_pre * slope).astype(jnp.bfloat16)
        grad_up = (back * gate_act).astype(jnp.bfloat16)
        first = head * 3 * width
        grad_ref[first : first + width, :] = product(grad_gate, keys, 0, 0).astype(jnp.bfloat16)
        grad_ref[first + width : first + 2 * width, :] = product(grad_up, keys, 0, 0).astype(
            jnp.bfloat16
        )
        grad_ref[first + 2 * width : first + 3 * width, :] = (
            -product(scaled, hidden, 0, 0)
        ).astype(jnp.bfloat16)


def local_gradient(own_count, token_keys, token_values, step_rates, fast_weights):
    heads, mats, width, _ = fast_weights.shape
    return pl.pallas_call(
        gradient_kernel,
        out_shape=jax.ShapeDtypeStruct((heads * mats * width, width), jnp.bfloat16),
        in_specs=[SMEM, VMEM, VMEM, VMEM, VMEM],
        out_specs=VMEM,
        name="gradient",
        compiler_params=pltpu.CompilerParams(vmem_limit_bytes=VMEM_BYTES),
        cost_estimate=pl.CostEstimate(
            flops=14 * 256 * width * width * heads, transcendentals=131072, bytes_accessed=3000000
        ),
    )(own_count, token_keys, token_values, step_rates, fast_weights)


def near_kernel(counts_ref, queries_ref, own_keys_ref, own_values_ref, near_ref, sum_ref, top_ref, mass_ref):
    tokens, heads, width = queries_ref.shape
    row = lax.broadcasted_iota(jnp.int32, (tokens, tokens), 0)
    column = lax.broadcasted_iota(jnp.int32, (tokens, tokens), 1)
    own_allowed = (column <= row) & (column < counts_ref[0])
    near_allowed = column < counts_ref[1]
    scale = 1.0 / math.sqrt(width)
    for head in range(heads):
        queries = queries_ref[:, head, :]
        own = product(queries, own_keys_ref[:, head, :], 1, 1) * scale
        near = product(queries, near_ref[0, :, head, :], 1, 1) * scale
        own = jnp.where(own_allowed, own, LOWEST)
        near = jnp.where(near_allowed, near, LOWEST)
        top = jnp.max(jnp.maximum(own, near), axis=1, keepdims=True)
        own, near = jnp.exp(own - top), jnp.exp(near - top)
        mass = jnp.sum(own + near, axis=1, keepdims=True)
        sum_ref[:, head * width : (head + 1) * width] = product(
            own.astype(jnp.bfloat16), own_values_ref[:, head, :], 1, 0
        ) + product(near.astype(jnp.bfloat16), near_ref[1, :, head, :], 1, 0)
        top_ref[head] = jnp.broadcast_to(top, top_ref.shape[1:])
        mass_ref[head] = jnp.broadcast_to(mass, mass_ref.shape[1:])


def near_attention(seen_counts, queries, token_keys, token_values, near):
    tokens, heads, width = queries.shape
    side = jax.ShapeDtypeStruct((heads, tokens, 128), jnp.float32)
    return pl.pallas_call(
        near_kernel,
        out_shape=(jax.ShapeDtypeStruct((tokens, heads * width), jnp.float32), side, side),
        in_specs=[SMEM, VMEM, VMEM, VMEM, VMEM],
        out_specs=(VMEM, VMEM, VMEM),
        name="near_attention",
        compiler_params=pltpu.CompilerParams(vmem_limit_bytes=VMEM_BYTES),
        cost_estimate=pl.CostEstimate(
            flops=8 * tokens * tokens * width * heads, transcendentals=262144, bytes_accessed=3000000
        ),
    )(seen_counts, queries, token_keys, token_values, near)


def feature_kernel(
    counts_ref, queries_ref, far_ref, sum_ref, top_ref, mass_ref, weights_ref, features_ref
):
    tokens, heads, width = queries_ref.shape
    row = lax.broadcasted_iota(jnp.int32, (tokens, tokens), 0)
    column = lax.broadcasted_iota(jnp.int32, (tokens, tokens), 1)
    far_allowed = (column > row) & (column < counts_ref[2])
    valid = lax.broadcasted_iota(jnp.int32, (tokens, 1), 0) < counts_ref[0]
    scale = 1.0 / math.sqrt(width)
    for head in range(heads):
        queries = queries_ref[:, head, :]
        far = product(queries, far_ref[0, :, head, :], 1, 1) * scale
        far = jnp.where(far_allowed, far, LOWEST)
        near_top = top_ref[head][:, :1]
        top = jnp.maximum(near_top, jnp.max(far, axis=1, keepdims=True))
        far = jnp.exp(far - top)
        kept = jnp.exp(near_top - top)
        mass = kept * mass_ref[head][:, :1] + jnp.sum(far, axis=1, keepdims=True)
        near_sum = sum_ref[:, head * width : (head + 1) * width]
        total = kept * near_sum + product(far.astype(jnp.bfloat16), far_ref[1, :, head, :], 1, 0)
        window = total / mass
        first = head * 3 * width
        gate = product(queries, weights_ref[first : first + width, :], 1, 1)
        up = product(queries, weights_ref[first + width : first + 2 * width, :], 1, 1)
        hidden = (gate * jax.nn.sigmoid(gate) * up).astype(jnp.bfloat16)
        learned = product(hidden, weights_ref[first + 2 * width : first + 3 * width, :], 1, 1)
        features_ref[:, head * width : (head + 1) * width] = jnp.where(
            valid, learned + window, 0.0
        ).astype(jnp.bfloat16)


def features_of(seen_counts, queries, far, near_sum, near_top, near_mass, new_flat):
    tokens, heads, width = queries.shape
    return pl.pallas_call(
        feature_kernel,
        out_shape=jax.ShapeDtypeStruct((tokens, heads * width), jnp.bfloat16),
        in_specs=[SMEM] + [VMEM] * 6,
        out_specs=VMEM,
        name="features",
        compiler_params=pltpu.CompilerParams(vmem_limit_bytes=VMEM_BYTES),
        cost_estimate=pl.CostEstimate(
            flops=10 * tokens * tokens * width * heads, transcendentals=262144, bytes_accessed=3000000
        ),
    )(seen_counts, queries, far, near_sum, near_top, near_mass, new_flat)


def project_kernel(place_ref, own_ref, other_ref, own_weight_ref, other_weight_ref, out_ref):
    out_ref[...] = (
        jnp.dot(own_ref[...], own_weight_ref[...], preferred_element_type=jnp.float32)
        + jnp.dot(other_ref[...], other_weight_ref[...], preferred_element_type=jnp.float32)
    ).astype(jnp.bfloat16)


def projected(head_place, own, other, own_weight, other_weight):
    tokens, depth = own.shape
    columns = other_weight.shape[1]
    tile = 512
    tiles = columns // tile
    return pl.pallas_call(
        project_kernel,
        out_shape=jax.ShapeDtypeStruct((tokens, columns), jnp.bfloat16),
        grid_spec=pltpu.PrefetchScalarGridSpec(
            num_scalar_prefetch=1,
            grid=(tiles,),
            in_specs=[
                pl.BlockSpec((tokens, depth), lambda step, place: (0, 0)),
                pl.BlockSpec((tokens, depth), lambda step, place: (0, 0)),
                pl.BlockSpec((depth, tile), lambda step, place: (0, place[0] * tiles + step)),
                pl.BlockSpec((depth, tile), lambda step, place: (0, step)),
            ],
            out_specs=pl.BlockSpec((tokens, tile), lambda step, place: (0, step)),
        ),
        name="project",
        cost_estimate=pl.CostEstimate(
            flops=4 * tokens * depth * columns, transcendentals=0, bytes_accessed=6000000
        ),
    )(head_place, own, other, own_weight, other_weight)


def refresh(old_rows, gradient_rows, token_total):
    updated = old_rows - gradient_rows / math.sqrt(token_total)
    old_norm = jnp.sqrt(jnp.sum(old_rows * old_rows, axis=-1, keepdims=True))
    fresh = (
        updated * old_norm / jnp.sqrt(jnp.sum(updated * updated, axis=-1, keepdims=True) + 1e-06)
    )
    return fresh.astype(jnp.bfloat16)


def shards(queries, token_keys, token_values, step_rates, counts, fast_weights, out_weight):
    tok_rows, _, head_width = queries.shape
    device_count, plane_count = lax.axis_size(CTX), lax.axis_size("p")
    device_place, head_place = lax.axis_index(CTX), lax.axis_index("head")
    places = device_place - jnp.arange(3, dtype=jnp.int32)
    seen_counts = jnp.where(places >= 0, counts[jnp.maximum(places, 0)], 0)
    pairs = jnp.stack([token_keys, token_values], 0)
    near = passed_along(pairs, 1)
    local_grad = local_gradient(
        seen_counts, token_keys, token_values, step_rates, fast_weights
    )
    blocks = lax.all_to_all(local_grad.reshape(device_count, -1, head_width), CTX, 0, 0, tiled=True)
    out_parts = out_weight.reshape(out_weight.shape[0], 2, -1)
    out_other = lax.ppermute(
        lax.dynamic_index_in_dim(out_parts, 1 - head_place, 1, keepdims=False),
        "head",
        [(0, 1), (1, 0)],
    )
    near_sum, near_top, near_mass = near_attention(
        seen_counts, queries, token_keys, token_values, near
    )
    grad_rows = jnp.sum(blocks.astype(jnp.float32), axis=0)
    own_rows = grad_rows.shape[0]
    old_rows = lax.dynamic_slice_in_dim(
        fast_weights.reshape(-1, head_width), device_place * own_rows, own_rows, 0
    )
    new_rows = refresh(old_rows, grad_rows, tok_rows * device_count)
    held = lax.all_to_all(
        jnp.broadcast_to(new_rows[None], (plane_count, *new_rows.shape)), "p", 0, 0, tiled=True
    )
    held = held.reshape(-1, head_width)
    pairs, held = lax.optimization_barrier((pairs, held))
    far = passed_along(pairs, 2)
    new_flat = lax.all_gather(held, "z", axis=0, tiled=True)
    features = features_of(
        seen_counts, queries, far, near_sum, near_top, near_mass, new_flat
    )
    other = lax.ppermute(features, "head", [(0, 1), (1, 0)])
    return projected(head_place.reshape(1), features, other, out_weight, out_other)


def solution(mesh):
    fine = Mesh(mesh.devices.reshape(RING, -1, 2), ("z", "p", "head"))
    in_specs = (
        P(CTX, "head", None),
        P(CTX, "head", None),
        P(CTX, "head", None),
        P(CTX, "head"),
        P(),
        P("head", None, None, None),
        P("head", None),
    )
    return jax.shard_map(
        shards, mesh=fine, in_specs=in_specs, out_specs=P(CTX, "head"), check_vma=False
    )
```

```python
import functools
import math

import jax
import jax.numpy as jnp
from jax import lax
from jax.experimental import pallas as pl
from jax.experimental.pallas import tpu as pltpu
from jax.sharding import Mesh, PartitionSpec as P


RING = 4
CTX = ("z", "p")
VMEM = pl.BlockSpec(memory_space=pltpu.VMEM)
SMEM = pl.BlockSpec(memory_space=pltpu.SMEM)
LOWEST = -1e30
VMEM_BYTES = 24 << 20


def passed_along(value, steps):
    count = lax.axis_size(CTX)
    return lax.ppermute(value, CTX, [(source, source + steps) for source in range(count - steps)])


def product(left, right, left_dim, right_dim):
    return lax.dot_general(
        left,
        right,
        (((left_dim,), (right_dim,)), ((), ())),
        preferred_element_type=jnp.float32,
    )


def place_count(counts_ref, place_ref, back_step):
    place = place_ref[0] - back_step
    return jnp.where(place >= 0, counts_ref[jnp.maximum(place, 0)], 0)


def chunked(rows):
    blocks = rows.shape[0] // 8
    left = rows[:, :128].reshape(blocks, 8, 128)
    right = rows[:, 128:].reshape(blocks, 8, 128)
    ahead = lax.broadcasted_iota(jnp.int32, (blocks, 8, 128), 1) < 4
    even = jnp.where(ahead, left, pltpu.roll(right, 4, 1))
    odd = jnp.where(ahead, pltpu.roll(left, 4, 1), right)
    return even.astype(jnp.bfloat16), odd.astype(jnp.bfloat16)


def gradient_kernel(place_ref, counts_ref, keys_ref, values_ref, rates_ref, weights_ref, grad_ref):
    tokens, heads, width = keys_ref.shape
    valid = lax.broadcasted_iota(jnp.int32, (tokens, 1), 0) < place_count(counts_ref, place_ref, 0)
    rates_all = jnp.concatenate(
        [rates_ref[...], jnp.zeros((8 - heads, tokens), jnp.float32)], 0
    ).T
    for head in range(heads):
        keys = keys_ref[:, head, :]
        values = values_ref[:, head, :].astype(jnp.float32)
        rates = jnp.where(valid, rates_all[:, head : head + 1], 0.0)
        scaled = (rates * values).astype(jnp.bfloat16)
        gate_weight = weights_ref[head, 0].astype(jnp.bfloat16)
        up_weight = weights_ref[head, 1].astype(jnp.bfloat16)
        down_weight = weights_ref[head, 2].astype(jnp.bfloat16)
        gate_pre = product(keys, gate_weight, 1, 1)
        up_pre = product(keys, up_weight, 1, 1)
        back = -product(scaled, down_weight, 1, 0)
        sigmoid = jax.nn.sigmoid(gate_pre)
        gate_act = gate_pre * sigmoid
        hidden = (gate_act * up_pre).astype(jnp.bfloat16)
        slope = sigmoid * (1.0 + gate_pre * (1.0 - sigmoid))
        grad_gate = (back * up_pre * slope).astype(jnp.bfloat16)
        grad_up = (back * gate_act).astype(jnp.bfloat16)
        mats = (
            product(grad_gate, keys, 0, 0),
            product(grad_up, keys, 0, 0),
            -product(scaled, hidden, 0, 0),
        )
        blocks = width // 8
        for index, mat in enumerate(mats):
            first = (head * 3 + index) * blocks
            even, odd = chunked(mat)
            grad_ref[first : first + blocks, 0] = even
            grad_ref[first : first + blocks, 1] = odd


def local_gradient(place, counts, token_keys, token_values, step_rates, fast_weights):
    heads, mats, width, _ = fast_weights.shape
    return pl.pallas_call(
        gradient_kernel,
        out_shape=jax.ShapeDtypeStruct((heads * mats * width // 8, 2, 8, 128), jnp.bfloat16),
        in_specs=[SMEM, SMEM, VMEM, VMEM, VMEM, VMEM],
        out_specs=VMEM,
        name="gradient",
        cost_estimate=pl.CostEstimate(
            flops=14 * 256 * width * width * heads, transcendentals=131072, bytes_accessed=3000000
        ),
    )(place, counts, token_keys, token_values, step_rates.T, fast_weights)


def own_kernel(
    place_ref, counts_ref, queries_ref, keys_ref, values_ref, pairs_ref, sum_ref, top_ref, mass_ref
):
    tokens, heads, width = queries_ref.shape
    row = lax.broadcasted_iota(jnp.int32, (tokens, tokens), 0)
    column = lax.broadcasted_iota(jnp.int32, (tokens, tokens), 1)
    allowed = (column <= row) & (column < place_count(counts_ref, place_ref, 0))
    scale = 1.0 / math.sqrt(width)
    for head in range(heads):
        keys, values = keys_ref[:, head, :], values_ref[:, head, :]
        pairs_ref[head] = keys
        pairs_ref[heads + head] = values
        own = product(queries_ref[:, head, :], keys, 1, 1) * scale
        own = jnp.where(allowed, own, LOWEST)
        top = jnp.max(own, axis=1, keepdims=True)
        own = jnp.exp(own - top)
        mass = jnp.sum(own, axis=1, keepdims=True)
        sum_ref[:, head * width : (head + 1) * width] = product(
            own.astype(jnp.bfloat16), values, 1, 0
        )
        top_ref[head] = jnp.broadcast_to(top, top_ref.shape[1:])
        mass_ref[head] = jnp.broadcast_to(mass, mass_ref.shape[1:])


def own_attention(place, counts, queries, token_keys, token_values):
    tokens, heads, width = queries.shape
    side = jax.ShapeDtypeStruct((heads, tokens, 128), jnp.float32)
    return pl.pallas_call(
        own_kernel,
        out_shape=(
            jax.ShapeDtypeStruct((2 * heads, tokens, width), jnp.bfloat16),
            jax.ShapeDtypeStruct((tokens, heads * width), jnp.float32),
            side,
            side,
        ),
        in_specs=[SMEM, SMEM, VMEM, VMEM, VMEM],
        out_specs=(VMEM, VMEM, VMEM, VMEM),
        name="own_attention",
        compiler_params=pltpu.CompilerParams(vmem_limit_bytes=VMEM_BYTES),
        cost_estimate=pl.CostEstimate(
            flops=4 * tokens * tokens * width * heads, transcendentals=131072, bytes_accessed=3000000
        ),
    )(place, counts, queries, token_keys, token_values)


def feature_kernel(
    place_ref,
    counts_ref,
    queries_ref,
    near_ref,
    far_ref,
    sum_ref,
    top_ref,
    mass_ref,
    weights_ref,
    features_ref,
):
    tokens, heads, width = queries_ref.shape
    row = lax.broadcasted_iota(jnp.int32, (tokens, tokens), 0)
    column = lax.broadcasted_iota(jnp.int32, (tokens, tokens), 1)
    near_allowed = column < place_count(counts_ref, place_ref, 1)
    far_allowed = (column > row) & (column < place_count(counts_ref, place_ref, 2))
    valid = lax.broadcasted_iota(jnp.int32, (tokens, 1), 0) < place_count(counts_ref, place_ref, 0)
    scale = 1.0 / math.sqrt(width)
    for head in range(heads):
        queries = queries_ref[:, head, :]
        near = product(queries, near_ref[head], 1, 1) * scale
        far = product(queries, far_ref[head], 1, 1) * scale
        near = jnp.where(near_allowed, near, LOWEST)
        far = jnp.where(far_allowed, far, LOWEST)
        own_top = top_ref[head][:, :1]
        top = jnp.maximum(own_top, jnp.max(jnp.maximum(near, far), axis=1, keepdims=True))
        near, far = jnp.exp(near - top), jnp.exp(far - top)
        kept = jnp.exp(own_top - top)
        mass = kept * mass_ref[head][:, :1] + jnp.sum(near + far, axis=1, keepdims=True)
        total = (
            kept * sum_ref[:, head * width : (head + 1) * width]
            + product(near.astype(jnp.bfloat16), near_ref[heads + head], 1, 0)
            + product(far.astype(jnp.bfloat16), far_ref[heads + head], 1, 0)
        )
        window = total / mass
        first = head * 3 * width
        gate = product(queries, weights_ref[first : first + width, :], 1, 1)
        up = product(queries, weights_ref[first + width : first + 2 * width, :], 1, 1)
        hidden = (gate * jax.nn.sigmoid(gate) * up).astype(jnp.bfloat16)
        learned = product(hidden, weights_ref[first + 2 * width : first + 3 * width, :], 1, 1)
        features_ref[:, head * width : (head + 1) * width] = jnp.where(
            valid, learned + window, 0.0
        ).astype(jnp.bfloat16)


def features_of(place, counts, queries, near, far, own_parts, new_flat):
    tokens, heads, width = queries.shape
    return pl.pallas_call(
        feature_kernel,
        out_shape=jax.ShapeDtypeStruct((tokens, heads * width), jnp.bfloat16),
        in_specs=[SMEM, SMEM] + [VMEM] * 7,
        out_specs=VMEM,
        name="features",
        compiler_params=pltpu.CompilerParams(vmem_limit_bytes=VMEM_BYTES),
        cost_estimate=pl.CostEstimate(
            flops=14 * tokens * tokens * width * heads,
            transcendentals=262144,
            bytes_accessed=3000000,
        ),
    )(place, counts, queries, near, far, *own_parts, new_flat)


def split_kernel(place_ref, mine_in_ref, theirs_in_ref, mine_ref, theirs_ref):
    mine_ref[...] = mine_in_ref[...]
    theirs_ref[...] = theirs_in_ref[...]


def column_halves(head_place, out_weight):
    depth, columns = out_weight.shape
    half = columns // 2
    tile = half // 2
    piece = jax.ShapeDtypeStruct((depth, half), out_weight.dtype)
    return pl.pallas_call(
        split_kernel,
        out_shape=(piece, piece),
        grid_spec=pltpu.PrefetchScalarGridSpec(
            num_scalar_prefetch=1,
            grid=(half // tile,),
            in_specs=[
                pl.BlockSpec((depth, tile), lambda step, place: (0, place[0] * 2 + step)),
                pl.BlockSpec((depth, tile), lambda step, place: (0, (1 - place[0]) * 2 + step)),
            ],
            out_specs=(
                pl.BlockSpec((depth, tile), lambda step, place: (0, step)),
                pl.BlockSpec((depth, tile), lambda step, place: (0, step)),
            ),
        ),
        name="split",
        compiler_params=pltpu.CompilerParams(vmem_limit_bytes=VMEM_BYTES),
        cost_estimate=pl.CostEstimate(flops=0, transcendentals=0, bytes_accessed=8000000),
    )(head_place, out_weight, out_weight)


def project_kernel(own_ref, other_ref, own_weight_ref, other_weight_ref, out_ref):
    out_ref[...] = (
        jnp.dot(own_ref[...], own_weight_ref[...], preferred_element_type=jnp.float32)
        + jnp.dot(other_ref[...], other_weight_ref[...], preferred_element_type=jnp.float32)
    ).astype(jnp.bfloat16)


def projected(own, other, own_weight, other_weight):
    tokens, depth = own.shape
    columns = other_weight.shape[1]
    tile = 512
    whole = pl.BlockSpec((tokens, depth), lambda step: (0, 0))
    piece = pl.BlockSpec((depth, tile), lambda step: (0, step))
    return pl.pallas_call(
        project_kernel,
        out_shape=jax.ShapeDtypeStruct((tokens, columns), jnp.bfloat16),
        grid=(columns // tile,),
        in_specs=[whole, whole, piece, piece],
        out_specs=pl.BlockSpec((tokens, tile), lambda step: (0, step)),
        name="project",
        compiler_params=pltpu.CompilerParams(vmem_limit_bytes=VMEM_BYTES),
        cost_estimate=pl.CostEstimate(
            flops=4 * tokens * depth * columns, transcendentals=0, bytes_accessed=6000000
        ),
    )(own, other, own_weight, other_weight)


def refresh_kernel(total, blocks_ref, old_ref, rows_ref):
    gradient = jnp.sum(blocks_ref[...].astype(jnp.float32), axis=0)
    gradient = jnp.concatenate([gradient[:4], gradient[4:]], 1)
    old = old_ref[...]
    updated = old - gradient / math.sqrt(total)
    old_norm = jnp.sqrt(jnp.sum(old * old, axis=1, keepdims=True))
    fresh = updated * old_norm / jnp.sqrt(jnp.sum(updated * updated, axis=1, keepdims=True) + 1e-06)
    rows_ref[...] = jnp.broadcast_to(fresh.astype(jnp.bfloat16)[None], rows_ref.shape)


def refreshed(total, copies, blocks, old_rows):
    return pl.pallas_call(
        functools.partial(refresh_kernel, total),
        out_shape=jax.ShapeDtypeStruct((copies, *old_rows.shape), jnp.bfloat16),
        in_specs=[VMEM, VMEM],
        out_specs=VMEM,
        name="refresh",
        compiler_params=pltpu.CompilerParams(vmem_limit_bytes=VMEM_BYTES),
        cost_estimate=pl.CostEstimate(flops=400000, transcendentals=0, bytes_accessed=1600000),
    )(blocks, old_rows)


def shards(queries, token_keys, token_values, step_rates, counts, fast_weights, out_weight):
    tok_rows, _, head_width = queries.shape
    device_count, plane_count = lax.axis_size(CTX), lax.axis_size("p")
    device_place, head_place = lax.axis_index(CTX), lax.axis_index("head")
    place = device_place.reshape(1).astype(jnp.int32)
    local_grad = local_gradient(place, counts, token_keys, token_values, step_rates, fast_weights)
    blocks = lax.all_to_all(local_grad.reshape(device_count, 8, 128), CTX, 0, 0, tiled=True)
    out_own, out_theirs = column_halves(
        head_place.reshape(1).astype(jnp.int32), out_weight
    )
    out_other = lax.ppermute(out_theirs, "head", [(0, 1), (1, 0)])
    pairs, *own_parts = own_attention(place, counts, queries, token_keys, token_values)
    old_flat = fast_weights.reshape(-1, head_width)
    own_rows = old_flat.shape[0] // device_count
    old_rows = lax.dynamic_slice_in_dim(old_flat, device_place * own_rows, own_rows, 0)
    new_rows = refreshed(tok_rows * device_count, plane_count, blocks, old_rows)
    held = lax.all_to_all(new_rows, "p", 0, 0, tiled=True)
    near = passed_along(pairs, 1)
    far = passed_along(pairs, 2)
    new_flat = lax.all_gather(held.reshape(-1, head_width), "z", axis=0, tiled=True)
    features = features_of(place, counts, queries, near, far, own_parts, new_flat)
    other = lax.ppermute(features, "head", [(0, 1), (1, 0)])
    return projected(features, other, out_own, out_other)


def solution(mesh):
    fine = Mesh(mesh.devices.reshape(RING, -1, 2), ("z", "p", "head"))
    in_specs = (
        P(CTX, "head", None),
        P(CTX, "head", None),
        P(CTX, "head", None),
        P(CTX, "head"),
        P(),
        P("head", None, None, None),
        P("head", None),
    )
    return jax.shard_map(
        shards, mesh=fine, in_specs=in_specs, out_specs=P(CTX, "head"), check_vma=False
    )
```

```python
import functools
import math

import jax
import jax.numpy as jnp
from jax import lax
from jax.experimental import pallas as pl
from jax.experimental.pallas import tpu as pltpu
from jax.sharding import Mesh, PartitionSpec as P


RING = 4
CTX = ("z", "p")
VMEM = pl.BlockSpec(memory_space=pltpu.VMEM)
SMEM = pl.BlockSpec(memory_space=pltpu.SMEM)
LOWEST = -1e30
VMEM_BYTES = 24 << 20


def passed_along(value, steps):
    count = lax.axis_size(CTX)
    return lax.ppermute(value, CTX, [(source, source + steps) for source in range(count - steps)])


def passed_in_plane(value):
    return lax.ppermute(value, "p", [(place, place + 1) for place in range(lax.axis_size("p") - 1)])


def turned(value, steps):
    return lax.ppermute(value, "z", [(place, (place + steps) % RING) for place in range(RING)])


def product(left, right, left_dim, right_dim):
    return lax.dot_general(
        left,
        right,
        (((left_dim,), (right_dim,)), ((), ())),
        preferred_element_type=jnp.float32,
    )


def place_count(counts_ref, place_ref, back_step):
    place = place_ref[0] - back_step
    return jnp.where(place >= 0, counts_ref[jnp.maximum(place, 0)], 0)


def chunked(rows):
    blocks = rows.shape[0] // 8
    left = rows[:, :128].reshape(blocks, 8, 128)
    right = rows[:, 128:].reshape(blocks, 8, 128)
    ahead = lax.broadcasted_iota(jnp.int32, (blocks, 8, 128), 1) < 4
    even = jnp.where(ahead, left, pltpu.roll(right, 4, 1))
    odd = jnp.where(ahead, pltpu.roll(left, 4, 1), right)
    return even.astype(jnp.bfloat16), odd.astype(jnp.bfloat16)


def gradient_kernel(
    place_ref, counts_ref, keys_ref, values_ref, rates_ref, weights_ref, *parts
):
    quarter_refs, (held_ref, sems) = parts[:RING], parts[RING:]
    tokens, heads, width = keys_ref.shape
    pieces = held_ref.shape[1]
    valid = lax.broadcasted_iota(jnp.int32, (tokens, 1), 0) < place_count(counts_ref, place_ref, 0)
    rates_all = jnp.concatenate(
        [rates_ref[...], jnp.zeros((8 - heads, tokens), jnp.float32)], 0
    ).T
    for head in range(heads):
        keys = keys_ref[:, head, :]
        values = values_ref[:, head, :].astype(jnp.float32)
        rates = jnp.where(valid, rates_all[:, head : head + 1], 0.0)
        scaled = (rates * values).astype(jnp.bfloat16)
        gate_weight = weights_ref[head, 0].astype(jnp.bfloat16)
        up_weight = weights_ref[head, 1].astype(jnp.bfloat16)
        down_weight = weights_ref[head, 2].astype(jnp.bfloat16)
        gate_pre = product(keys, gate_weight, 1, 1)
        up_pre = product(keys, up_weight, 1, 1)
        back = -product(scaled, down_weight, 1, 0)
        sigmoid = jax.nn.sigmoid(gate_pre)
        gate_act = gate_pre * sigmoid
        hidden = (gate_act * up_pre).astype(jnp.bfloat16)
        slope = sigmoid * (1.0 + gate_pre * (1.0 - sigmoid))
        grad_gate = (back * up_pre * slope).astype(jnp.bfloat16)
        grad_up = (back * gate_act).astype(jnp.bfloat16)
        mats = (
            product(grad_gate, keys, 0, 0),
            product(grad_up, keys, 0, 0),
            -product(scaled, hidden, 0, 0),
        )
        half = width // 16
        for index, mat in enumerate(mats):
            even, odd = chunked(mat)
            for side in range(2):
                piece = (head * 3 + index) * 2 + side
                rows = slice(side * half, (side + 1) * half)
                held_ref[piece // pieces, piece % pieces, :, 0] = even[rows]
                held_ref[piece // pieces, piece % pieces, :, 1] = odd[rows]
    ring_place = place_ref[1]
    copies = [
        pltpu.make_async_copy(
            held_ref.at[lax.rem(ring_place + steps, RING)], quarter_refs[steps], sems.at[steps]
        )
        for steps in range(RING)
    ]
    for copy in copies:
        copy.start()
    for copy in copies:
        copy.wait()


def local_gradient(place, counts, token_keys, token_values, step_rates, fast_weights):
    heads, mats, width, _ = fast_weights.shape
    shape = (2 * heads * mats // RING, width // 16, 2, 8, 128)
    quarter = jax.ShapeDtypeStruct(shape, jnp.bfloat16)
    return pl.pallas_call(
        gradient_kernel,
        out_shape=(quarter,) * RING,
        in_specs=[SMEM, SMEM, VMEM, VMEM, VMEM, VMEM],
        out_specs=(pl.BlockSpec(memory_space=pl.ANY),) * RING,
        scratch_shapes=[
            pltpu.VMEM((RING, *shape), jnp.bfloat16),
            pltpu.SemaphoreType.DMA((RING,)),
        ],
        name="gradient",
        cost_estimate=pl.CostEstimate(
            flops=14 * 256 * width * width * heads, transcendentals=131072, bytes_accessed=3000000
        ),
    )(place, counts, token_keys, token_values, step_rates.T, fast_weights)


def pair_kernel(keys_ref, values_ref, pairs_ref):
    heads = keys_ref.shape[1]
    for head in range(heads):
        pairs_ref[head] = keys_ref[:, head, :]
        pairs_ref[heads + head] = values_ref[:, head, :]


def paired(token_keys, token_values):
    tokens, heads, width = token_keys.shape
    return pl.pallas_call(
        pair_kernel,
        out_shape=jax.ShapeDtypeStruct((2 * heads, tokens, width), jnp.bfloat16),
        in_specs=[VMEM, VMEM],
        out_specs=VMEM,
        name="pair",
        cost_estimate=pl.CostEstimate(flops=0, transcendentals=0, bytes_accessed=2000000),
    )(token_keys, token_values)


def own_kernel(place_ref, counts_ref, queries_ref, pairs_ref, state_ref):
    tokens, heads, width = queries_ref.shape
    row = lax.broadcasted_iota(jnp.int32, (tokens, tokens), 0)
    column = lax.broadcasted_iota(jnp.int32, (tokens, tokens), 1)
    allowed = (column <= row) & (column < place_count(counts_ref, place_ref, 0))
    scale = 1.0 / math.sqrt(width)
    for head in range(heads):
        own = product(queries_ref[:, head, :], pairs_ref[head], 1, 1) * scale
        own = jnp.where(allowed, own, LOWEST)
        top = jnp.max(own, axis=1, keepdims=True)
        own = jnp.exp(own - top)
        mass = jnp.sum(own, axis=1, keepdims=True)
        state_ref[head, :, :width] = product(
            own.astype(jnp.bfloat16), pairs_ref[heads + head], 1, 0
        )
        state_ref[head, :, width : width + 128] = jnp.broadcast_to(top, (tokens, 128))
        state_ref[head, :, width + 128 :] = jnp.broadcast_to(mass, (tokens, 128))


def own_attention(place, counts, queries, pairs):
    tokens, heads, width = queries.shape
    return pl.pallas_call(
        own_kernel,
        out_shape=jax.ShapeDtypeStruct((heads, tokens, width + 256), jnp.float32),
        in_specs=[SMEM, SMEM, VMEM, VMEM],
        out_specs=VMEM,
        name="own_attention",
        compiler_params=pltpu.CompilerParams(vmem_limit_bytes=VMEM_BYTES),
        cost_estimate=pl.CostEstimate(
            flops=4 * tokens * tokens * width * heads, transcendentals=131072, bytes_accessed=3000000
        ),
    )(place, counts, queries, pairs)


def feature_kernel(
    place_ref,
    counts_ref,
    queries_ref,
    near_ref,
    first_ref,
    far_ref,
    state_ref,
    weights_ref,
    features_ref,
):
    tokens, heads, width = queries_ref.shape
    row = lax.broadcasted_iota(jnp.int32, (tokens, tokens), 0)
    column = lax.broadcasted_iota(jnp.int32, (tokens, tokens), 1)
    near_allowed = column < place_count(counts_ref, place_ref, 1)
    far_allowed = (column > row) & (column < place_count(counts_ref, place_ref, 2))
    valid = lax.broadcasted_iota(jnp.int32, (tokens, 1), 0) < place_count(counts_ref, place_ref, 0)
    scale = 1.0 / math.sqrt(width)
    at_start = place_ref[2] == 0
    for head in range(heads):
        queries = queries_ref[:, head, :]
        near_keys = jnp.where(at_start, first_ref[head], near_ref[head])
        near_values = jnp.where(at_start, first_ref[heads + head], near_ref[heads + head])
        near = product(queries, near_keys, 1, 1) * scale
        far = product(queries, far_ref[head], 1, 1) * scale
        near = jnp.where(near_allowed, near, LOWEST)
        far = jnp.where(far_allowed, far, LOWEST)
        own_top = state_ref[head, :, width : width + 1]
        own_mass = state_ref[head, :, width + 128 : width + 129]
        top = jnp.maximum(own_top, jnp.max(jnp.maximum(near, far), axis=1, keepdims=True))
        near, far = jnp.exp(near - top), jnp.exp(far - top)
        kept = jnp.exp(own_top - top)
        mass = kept * own_mass + jnp.sum(near + far, axis=1, keepdims=True)
        total = (
            kept * state_ref[head, :, :width]
            + product(near.astype(jnp.bfloat16), near_values, 1, 0)
            + product(far.astype(jnp.bfloat16), far_ref[heads + head], 1, 0)
        )
        window = total / mass
        first = head * 3 * width
        gate = product(queries, weights_ref[first : first + width, :], 1, 1)
        up = product(queries, weights_ref[first + width : first + 2 * width, :], 1, 1)
        hidden = (gate * jax.nn.sigmoid(gate) * up).astype(jnp.bfloat16)
        learned = product(hidden, weights_ref[first + 2 * width : first + 3 * width, :], 1, 1)
        features_ref[:, head * width : (head + 1) * width] = jnp.where(
            valid, learned + window, 0.0
        ).astype(jnp.bfloat16)


def features_of(place, counts, queries, near, first, far, state, new_flat):
    tokens, heads, width = queries.shape
    return pl.pallas_call(
        feature_kernel,
        out_shape=jax.ShapeDtypeStruct((tokens, heads * width), jnp.bfloat16),
        in_specs=[SMEM, SMEM] + [VMEM] * 6,
        out_specs=VMEM,
        name="features",
        compiler_params=pltpu.CompilerParams(vmem_limit_bytes=VMEM_BYTES),
        cost_estimate=pl.CostEstimate(
            flops=14 * tokens * tokens * width * heads,
            transcendentals=262144,
            bytes_accessed=3000000,
        ),
    )(place, counts, queries, near, first, far, state, new_flat)


def split_kernel(place_ref, mine_in_ref, theirs_in_ref, mine_ref, theirs_ref):
    mine_ref[...] = mine_in_ref[...]
    theirs_ref[...] = theirs_in_ref[...]


def column_halves(head_place, out_weight):
    depth, columns = out_weight.shape
    half = columns // 2
    tile = half // 2
    piece = jax.ShapeDtypeStruct((depth, half), out_weight.dtype)
    return pl.pallas_call(
        split_kernel,
        out_shape=(piece, piece),
        grid_spec=pltpu.PrefetchScalarGridSpec(
            num_scalar_prefetch=1,
            grid=(half // tile,),
            in_specs=[
                pl.BlockSpec((depth, tile), lambda step, place: (0, place[0] * 2 + step)),
                pl.BlockSpec((depth, tile), lambda step, place: (0, (1 - place[0]) * 2 + step)),
            ],
            out_specs=(
                pl.BlockSpec((depth, tile), lambda step, place: (0, step)),
                pl.BlockSpec((depth, tile), lambda step, place: (0, step)),
            ),
        ),
        name="split",
        compiler_params=pltpu.CompilerParams(vmem_limit_bytes=VMEM_BYTES),
        cost_estimate=pl.CostEstimate(flops=0, transcendentals=0, bytes_accessed=8000000),
    )(head_place, out_weight, out_weight)


def own_project_kernel(own_ref, weight_ref, out_ref):
    out_ref[...] = jnp.dot(own_ref[...], weight_ref[...], preferred_element_type=jnp.float32)


def own_projected(own, weight):
    return pl.pallas_call(
        own_project_kernel,
        out_shape=jax.ShapeDtypeStruct((own.shape[0], weight.shape[1]), jnp.float32),
        in_specs=[VMEM, VMEM],
        out_specs=VMEM,
        name="own_project",
        compiler_params=pltpu.CompilerParams(vmem_limit_bytes=VMEM_BYTES),
        cost_estimate=pl.CostEstimate(
            flops=2 * own.shape[0] * weight.size, transcendentals=0, bytes_accessed=4000000
        ),
    )(own, weight)


def project_kernel(other_ref, weight_ref, own_ref, out_ref):
    out_ref[...] = (
        own_ref[...]
        + jnp.dot(other_ref[...], weight_ref[...], preferred_element_type=jnp.float32)
    ).astype(jnp.bfloat16)


def projected(other, weight, own_product):
    tokens, depth = other.shape
    columns = weight.shape[1]
    tile = columns // 2
    return pl.pallas_call(
        project_kernel,
        out_shape=jax.ShapeDtypeStruct((tokens, columns), jnp.bfloat16),
        grid=(columns // tile,),
        in_specs=[
            pl.BlockSpec((tokens, depth), lambda step: (0, 0)),
            pl.BlockSpec((depth, tile), lambda step: (0, step)),
            pl.BlockSpec((tokens, tile), lambda step: (0, step)),
        ],
        out_specs=pl.BlockSpec((tokens, tile), lambda step: (0, step)),
        name="project",
        compiler_params=pltpu.CompilerParams(vmem_limit_bytes=VMEM_BYTES),
        cost_estimate=pl.CostEstimate(
            flops=2 * tokens * depth * columns, transcendentals=0, bytes_accessed=6000000
        ),
    )(other, weight, own_product)


def refresh_kernel(total, blocks_ref, old_ref, rows_ref):
    gradient = jnp.sum(blocks_ref[...].astype(jnp.float32), axis=0)
    gradient = jnp.concatenate([gradient[:4], gradient[4:]], 1)
    old = old_ref[...]
    updated = old - gradient / math.sqrt(total)
    old_norm = jnp.sqrt(jnp.sum(old * old, axis=1, keepdims=True))
    fresh = updated * old_norm / jnp.sqrt(jnp.sum(updated * updated, axis=1, keepdims=True) + 1e-06)
    rows_ref[...] = jnp.broadcast_to(fresh.astype(jnp.bfloat16)[None], rows_ref.shape)


def refreshed(total, copies, blocks, old_rows):
    return pl.pallas_call(
        functools.partial(refresh_kernel, total),
        out_shape=jax.ShapeDtypeStruct((copies, *old_rows.shape), jnp.bfloat16),
        in_specs=[VMEM, VMEM],
        out_specs=VMEM,
        name="refresh",
        compiler_params=pltpu.CompilerParams(vmem_limit_bytes=VMEM_BYTES),
        cost_estimate=pl.CostEstimate(flops=400000, transcendentals=0, bytes_accessed=1600000),
    )(blocks, old_rows)


def shards(queries, token_keys, token_values, step_rates, counts, fast_weights, out_weight):
    tok_rows, _, head_width = queries.shape
    device_count, plane_count = lax.axis_size(CTX), lax.axis_size("p")
    device_place, head_place = lax.axis_index(CTX), lax.axis_index("head")
    place = jnp.stack([device_place, lax.axis_index("z"), lax.axis_index("p"), head_place])
    place = place.astype(jnp.int32)
    pairs = paired(token_keys, token_values)
    far = passed_along(pairs, 2)
    quarters = local_gradient(
        place, counts, token_keys, token_values, step_rates, fast_weights
    )
    arrived = []
    for steps in range(1, RING):
        arrived.append(turned(quarters[steps], steps))
    summed = quarters[0].astype(jnp.float32)
    for part in arrived:
        summed = summed + part.astype(jnp.float32)
    summed = summed.astype(jnp.bfloat16).reshape(plane_count, 8, 128)
    blocks = lax.all_to_all(summed, "p", 0, 0, tiled=True)
    out_own, out_theirs = column_halves(place[3:], out_weight)
    out_other = lax.ppermute(out_theirs, "head", [(0, 1), (1, 0)])
    state = own_attention(place, counts, queries, pairs)
    old_flat = fast_weights.reshape(-1, head_width)
    own_rows = old_flat.shape[0] // device_count
    old_rows = lax.dynamic_slice_in_dim(old_flat, device_place * own_rows, own_rows, 0)
    new_rows = refreshed(tok_rows * device_count, plane_count, blocks, old_rows)
    held = lax.all_to_all(new_rows, "p", 0, 0, tiled=True)
    first = lax.ppermute(far, "p", [(1, 0)])
    near = passed_in_plane(pairs)
    new_flat = lax.all_gather(held.reshape(-1, head_width), "z", axis=0, tiled=True)
    features = features_of(place, counts, queries, near, first, far, state, new_flat)
    other = lax.ppermute(features, "head", [(0, 1), (1, 0)])
    own_product = own_projected(features, out_own)
    return projected(other, out_other, own_product)


def solution(mesh):
    fine = Mesh(mesh.devices.reshape(RING, -1, 2), ("z", "p", "head"))
    in_specs = (
        P(CTX, "head", None),
        P(CTX, "head", None),
        P(CTX, "head", None),
        P(CTX, "head"),
        P(),
        P("head", None, None, None),
        P("head", None),
    )
    return jax.shard_map(
        shards, mesh=fine, in_specs=in_specs, out_specs=P(CTX, "head"), check_vma=False
    )
```

```python
import functools
import math

import jax
import jax.numpy as jnp
from jax import lax
from jax.experimental import pallas as pl
from jax.experimental.pallas import tpu as pltpu
from jax.sharding import Mesh, PartitionSpec as P


RING = 4
CTX = ("z", "p")
VMEM = pl.BlockSpec(memory_space=pltpu.VMEM)
SMEM = pl.BlockSpec(memory_space=pltpu.SMEM)
LOWEST = -1e30
VMEM_BYTES = 24 << 20


def passed_along(value, steps):
    count = lax.axis_size(CTX)
    return lax.ppermute(value, CTX, [(source, source + steps) for source in range(count - steps)])


def product(left, right, left_dim, right_dim):
    return lax.dot_general(
        left,
        right,
        (((left_dim,), (right_dim,)), ((), ())),
        preferred_element_type=jnp.float32,
    )


def place_count(counts_ref, place_ref, back_step):
    place = place_ref[0] - back_step
    return jnp.where(place >= 0, counts_ref[jnp.maximum(place, 0)], 0)


def gradient_kernel(
    place_ref, counts_ref, keys_ref, values_ref, rates_ref, weights_ref, grad_ref, pairs_ref
):
    tokens, heads, width = keys_ref.shape
    valid = lax.broadcasted_iota(jnp.int32, (tokens, 1), 0) < place_count(counts_ref, place_ref, 0)
    rates_all = jnp.concatenate(
        [rates_ref[...], jnp.zeros((8 - heads, tokens), jnp.float32)], 0
    ).T
    for head in range(heads):
        keys, values = keys_ref[:, head, :], values_ref[:, head, :]
        pairs_ref[head] = keys
        pairs_ref[heads + head] = values
        rates = jnp.where(valid, rates_all[:, head : head + 1], 0.0)
        scaled = (rates * values.astype(jnp.float32)).astype(jnp.bfloat16)
        gate_weight = weights_ref[head, 0].astype(jnp.bfloat16)
        up_weight = weights_ref[head, 1].astype(jnp.bfloat16)
        down_weight = weights_ref[head, 2].astype(jnp.bfloat16)
        gate_pre = product(keys, gate_weight, 1, 1)
        up_pre = product(keys, up_weight, 1, 1)
        back = -product(scaled, down_weight, 1, 0)
        sigmoid = jax.nn.sigmoid(gate_pre)
        gate_act = gate_pre * sigmoid
        hidden = (gate_act * up_pre).astype(jnp.bfloat16)
        slope = sigmoid * (1.0 + gate_pre * (1.0 - sigmoid))
        grad_gate = (back * up_pre * slope).astype(jnp.bfloat16)
        grad_up = (back * gate_act).astype(jnp.bfloat16)
        mats = (
            product(grad_gate, keys, 0, 0),
            product(grad_up, keys, 0, 0),
            -product(scaled, hidden, 0, 0),
        )
        for index, mat in enumerate(mats):
            first = (head * 3 + index) * width
            grad_ref[first : first + width, :] = mat.astype(jnp.bfloat16)


def local_gradient(place, counts, token_keys, token_values, step_rates, fast_weights):
    heads, mats, width, _ = fast_weights.shape
    return pl.pallas_call(
        gradient_kernel,
        out_shape=(
            jax.ShapeDtypeStruct((heads * mats * width, width), jnp.bfloat16),
            jax.ShapeDtypeStruct((2 * heads, token_keys.shape[0], width), jnp.bfloat16),
        ),
        in_specs=[SMEM, SMEM, VMEM, VMEM, VMEM, VMEM],
        out_specs=(VMEM, VMEM),
        name="gradient",
        cost_estimate=pl.CostEstimate(
            flops=14 * 256 * width * width * heads, transcendentals=131072, bytes_accessed=3000000
        ),
    )(place, counts, token_keys, token_values, step_rates.T, fast_weights)


def window_kernel(place_ref, counts_ref, queries_ref, own_ref, near_ref, far_ref, window_ref, turned_ref):
    tokens, heads, width = queries_ref.shape
    row = lax.broadcasted_iota(jnp.int32, (tokens, tokens), 0)
    column = lax.broadcasted_iota(jnp.int32, (tokens, tokens), 1)
    blocks = (
        (own_ref, (column <= row) & (column < place_count(counts_ref, place_ref, 0))),
        (near_ref, column < place_count(counts_ref, place_ref, 1)),
        (far_ref, (column > row) & (column < place_count(counts_ref, place_ref, 2))),
    )
    scale = 1.0 / math.sqrt(width)
    for head in range(heads):
        queries = queries_ref[:, head, :]
        turned_ref[head] = queries
        scores = [
            jnp.where(allowed, product(queries, block[head], 1, 1) * scale, LOWEST)
            for block, allowed in blocks
        ]
        top = jnp.max(functools.reduce(jnp.maximum, scores), axis=1, keepdims=True)
        expo = [jnp.exp(score - top) for score in scores]
        mass = jnp.sum(sum(expo), axis=1, keepdims=True)
        total = sum(
            product(part.astype(jnp.bfloat16), block[heads + head], 1, 0)
            for part, (block, _) in zip(expo, blocks)
        )
        window_ref[:, head * width : (head + 1) * width] = total / mass


def window_attention(place, counts, queries, own, near, far):
    tokens, heads, width = queries.shape
    return pl.pallas_call(
        window_kernel,
        out_shape=(
            jax.ShapeDtypeStruct((tokens, heads * width), jnp.float32),
            jax.ShapeDtypeStruct((heads, tokens, width), jnp.bfloat16),
        ),
        in_specs=[SMEM, SMEM] + [VMEM] * 4,
        out_specs=(VMEM, VMEM),
        name="window",
        compiler_params=pltpu.CompilerParams(vmem_limit_bytes=VMEM_BYTES),
        cost_estimate=pl.CostEstimate(
            flops=12 * tokens * tokens * width * heads,
            transcendentals=400000,
            bytes_accessed=3000000,
        ),
    )(place, counts, queries, own, near, far)


def feature_kernel(place_ref, counts_ref, queries_ref, window_ref, weights_ref, features_ref):
    heads, tokens, width = queries_ref.shape
    valid = lax.broadcasted_iota(jnp.int32, (tokens, 1), 0) < place_count(counts_ref, place_ref, 0)
    for head in range(heads):
        queries = queries_ref[head]
        first = head * 3 * width
        gate = product(queries, weights_ref[first : first + width, :], 1, 1)
        up = product(queries, weights_ref[first + width : first + 2 * width, :], 1, 1)
        hidden = (gate * jax.nn.sigmoid(gate) * up).astype(jnp.bfloat16)
        learned = product(hidden, weights_ref[first + 2 * width : first + 3 * width, :], 1, 1)
        columns = slice(head * width, (head + 1) * width)
        features_ref[:, columns] = jnp.where(
            valid, learned + window_ref[:, columns], 0.0
        ).astype(jnp.bfloat16)


def features_of(place, counts, queries, window, new_flat):
    heads, tokens, width = queries.shape
    return pl.pallas_call(
        feature_kernel,
        out_shape=jax.ShapeDtypeStruct((tokens, heads * width), jnp.bfloat16),
        in_specs=[SMEM, SMEM] + [VMEM] * 3,
        out_specs=VMEM,
        name="features",
        compiler_params=pltpu.CompilerParams(vmem_limit_bytes=VMEM_BYTES),
        cost_estimate=pl.CostEstimate(
            flops=6 * tokens * width * width * heads, transcendentals=131072, bytes_accessed=2000000
        ),
    )(place, counts, queries, window, new_flat)


def split_kernel(place_ref, mine_in_ref, theirs_in_ref, mine_ref, theirs_ref):
    mine_ref[...] = mine_in_ref[...]
    theirs_ref[...] = theirs_in_ref[...]


def column_halves(head_place, out_weight):
    depth, columns = out_weight.shape
    half = columns // 2
    tile = half // 2
    piece = jax.ShapeDtypeStruct((depth, half), out_weight.dtype)
    return pl.pallas_call(
        split_kernel,
        out_shape=(piece, piece),
        grid_spec=pltpu.PrefetchScalarGridSpec(
            num_scalar_prefetch=1,
            grid=(half // tile,),
            in_specs=[
                pl.BlockSpec((depth, tile), lambda step, place: (0, place[0] * 2 + step)),
                pl.BlockSpec((depth, tile), lambda step, place: (0, (1 - place[0]) * 2 + step)),
            ],
            out_specs=(
                pl.BlockSpec((depth, tile), lambda step, place: (0, step)),
                pl.BlockSpec((depth, tile), lambda step, place: (0, step)),
            ),
        ),
        name="split",
        compiler_params=pltpu.CompilerParams(vmem_limit_bytes=VMEM_BYTES),
        cost_estimate=pl.CostEstimate(flops=0, transcendentals=0, bytes_accessed=8000000),
    )(head_place, out_weight, out_weight)


def own_project_kernel(own_ref, weight_ref, out_ref):
    out_ref[...] = jnp.dot(own_ref[...], weight_ref[...], preferred_element_type=jnp.float32)


def own_projected(own, weight):
    return pl.pallas_call(
        own_project_kernel,
        out_shape=jax.ShapeDtypeStruct((own.shape[0], weight.shape[1]), jnp.float32),
        in_specs=[VMEM, VMEM],
        out_specs=VMEM,
        name="own_project",
        compiler_params=pltpu.CompilerParams(vmem_limit_bytes=VMEM_BYTES),
        cost_estimate=pl.CostEstimate(
            flops=2 * own.shape[0] * weight.size, transcendentals=0, bytes_accessed=4000000
        ),
    )(own, weight)


def project_kernel(other_ref, weight_ref, own_ref, out_ref):
    out_ref[...] = (
        own_ref[...]
        + jnp.dot(other_ref[...], weight_ref[...], preferred_element_type=jnp.float32)
    ).astype(jnp.bfloat16)


def projected(other, weight, own_product):
    tokens, depth = other.shape
    columns = weight.shape[1]
    tile = columns // 2
    return pl.pallas_call(
        project_kernel,
        out_shape=jax.ShapeDtypeStruct((tokens, columns), jnp.bfloat16),
        grid=(columns // tile,),
        in_specs=[
            pl.BlockSpec((tokens, depth), lambda step: (0, 0)),
            pl.BlockSpec((depth, tile), lambda step: (0, step)),
            pl.BlockSpec((tokens, tile), lambda step: (0, step)),
        ],
        out_specs=pl.BlockSpec((tokens, tile), lambda step: (0, step)),
        name="project",
        compiler_params=pltpu.CompilerParams(vmem_limit_bytes=VMEM_BYTES),
        cost_estimate=pl.CostEstimate(
            flops=2 * tokens * depth * columns, transcendentals=0, bytes_accessed=6000000
        ),
    )(other, weight, own_product)


def collect_kernel(blocks_ref, sums_ref):
    total = jnp.sum(blocks_ref[...].astype(jnp.float32), axis=0)
    sums_ref[...] = jnp.broadcast_to(total[None], sums_ref.shape)


def collected(copies, blocks):
    return pl.pallas_call(
        collect_kernel,
        out_shape=jax.ShapeDtypeStruct((copies, *blocks.shape[1:]), jnp.float32),
        in_specs=[VMEM],
        out_specs=VMEM,
        name="collect",
        compiler_params=pltpu.CompilerParams(vmem_limit_bytes=VMEM_BYTES),
        cost_estimate=pl.CostEstimate(flops=400000, transcendentals=0, bytes_accessed=800000),
    )(blocks)


def refresh_kernel(total, sums_ref, old_ref, rows_ref):
    gradient = jnp.sum(sums_ref[...], axis=0)
    old = old_ref[...]
    updated = old - gradient / math.sqrt(total)
    old_norm = jnp.sqrt(jnp.sum(old * old, axis=1, keepdims=True))
    fresh = updated * old_norm / jnp.sqrt(jnp.sum(updated * updated, axis=1, keepdims=True) + 1e-06)
    rows_ref[...] = jnp.broadcast_to(fresh.astype(jnp.bfloat16)[None], rows_ref.shape)


def refreshed(total, copies, sums, old_rows):
    return pl.pallas_call(
        functools.partial(refresh_kernel, total),
        out_shape=jax.ShapeDtypeStruct((copies, *old_rows.shape), jnp.bfloat16),
        in_specs=[VMEM, VMEM],
        out_specs=VMEM,
        name="refresh",
        compiler_params=pltpu.CompilerParams(vmem_limit_bytes=VMEM_BYTES),
        cost_estimate=pl.CostEstimate(flops=100000, transcendentals=0, bytes_accessed=1000000),
    )(sums, old_rows)


def shards(queries, token_keys, token_values, step_rates, counts, fast_weights, out_weight):
    tok_rows, _, head_width = queries.shape
    device_count, plane_count = lax.axis_size(CTX), lax.axis_size("p")
    plane_place, head_place = lax.axis_index("p"), lax.axis_index("head")
    place = lax.axis_index(CTX).reshape(1).astype(jnp.int32)
    local_grad, pairs = local_gradient(
        place, counts, token_keys, token_values, step_rates, fast_weights
    )
    near = passed_along(pairs, 1)
    blocks = lax.all_to_all(local_grad.reshape(plane_count, -1, head_width), "p", 0, 0, tiled=True)
    out_own, out_theirs = column_halves(
        head_place.reshape(1).astype(jnp.int32), out_weight
    )
    out_other = lax.ppermute(out_theirs, "head", [(0, 1), (1, 0)])
    sums = collected(RING, blocks)
    sums = lax.all_to_all(sums, "z", 0, 0, tiled=True)
    far = passed_along(pairs, 2)
    old_flat = fast_weights.reshape(-1, head_width)
    own_rows = old_flat.shape[0] // plane_count
    old_rows = lax.dynamic_slice_in_dim(old_flat, plane_place * own_rows, own_rows, 0)
    new_rows = refreshed(tok_rows * device_count, plane_count, sums, old_rows)
    new_flat = lax.all_to_all(new_rows, "p", 0, 0, tiled=True).reshape(-1, head_width)
    window, turned_queries = window_attention(place, counts, queries, pairs, near, far)
    features = features_of(place, counts, turned_queries, window, new_flat)
    other = lax.ppermute(features, "head", [(0, 1), (1, 0)])
    own_product = own_projected(features, out_own)
    return projected(other, out_other, own_product)


def solution(mesh):
    fine = Mesh(mesh.devices.reshape(RING, -1, 2), ("z", "p", "head"))
    in_specs = (
        P(CTX, "head", None),
        P(CTX, "head", None),
        P(CTX, "head", None),
        P(CTX, "head"),
        P(),
        P("head", None, None, None),
        P("head", None),
    )
    return jax.shard_map(
        shards, mesh=fine, in_specs=in_specs, out_specs=P(CTX, "head"), check_vma=False
    )
```

```python
import functools
import math

import jax
import jax.numpy as jnp
from jax import lax
from jax.experimental import pallas as pl
from jax.experimental.pallas import tpu as pltpu
from jax.sharding import Mesh, PartitionSpec as P


RING = 4
CTX = ("z", "p")
VMEM = pl.BlockSpec(memory_space=pltpu.VMEM)
SMEM = pl.BlockSpec(memory_space=pltpu.SMEM)
LOWEST = -1e30
VMEM_BYTES = 24 << 20


def passed_along(value, steps):
    count = lax.axis_size(CTX)
    return lax.ppermute(value, CTX, [(source, source + steps) for source in range(count - steps)])


def product(left, right, left_dim, right_dim):
    return lax.dot_general(
        left,
        right,
        (((left_dim,), (right_dim,)), ((), ())),
        preferred_element_type=jnp.float32,
    )


def place_count(counts_ref, place_ref, back_step):
    place = place_ref[0] - back_step
    return jnp.where(place >= 0, counts_ref[jnp.maximum(place, 0)], 0)


def gradient_kernel(
    place_ref, counts_ref, keys_ref, values_ref, rates_ref, weights_ref, grad_ref, pairs_ref
):
    tokens, heads, width = keys_ref.shape

    def one_head(head):
        valid = lax.broadcasted_iota(jnp.int32, (tokens, 1), 0) < place_count(
            counts_ref, place_ref, 0
        )
        rates_all = jnp.concatenate(
            [rates_ref[...], jnp.zeros((8 - heads, tokens), jnp.float32)], 0
        ).T
        keys, values = keys_ref[:, head, :], values_ref[:, head, :]
        pairs_ref[0, 0] = keys
        pairs_ref[1, 0] = values
        rates = jnp.where(valid, rates_all[:, head : head + 1], 0.0)
        scaled = (rates * values.astype(jnp.float32)).astype(jnp.bfloat16)
        gate_weight = weights_ref[0, 0].astype(jnp.bfloat16)
        up_weight = weights_ref[0, 1].astype(jnp.bfloat16)
        down_weight = weights_ref[0, 2].astype(jnp.bfloat16)
        gate_pre = product(keys, gate_weight, 1, 1)
        up_pre = product(keys, up_weight, 1, 1)
        back = -product(scaled, down_weight, 1, 0)
        sigmoid = jax.nn.sigmoid(gate_pre)
        gate_act = gate_pre * sigmoid
        hidden = (gate_act * up_pre).astype(jnp.bfloat16)
        slope = sigmoid * (1.0 + gate_pre * (1.0 - sigmoid))
        grad_gate = (back * up_pre * slope).astype(jnp.bfloat16)
        grad_up = (back * gate_act).astype(jnp.bfloat16)
        mats = (
            product(grad_gate, keys, 0, 0),
            product(grad_up, keys, 0, 0),
            -product(scaled, hidden, 0, 0),
        )
        for index, mat in enumerate(mats):
            grad_ref[index * width : (index + 1) * width, :] = mat.astype(jnp.bfloat16)

    for head in range(heads):
        pl.when(pl.program_id(0) == head)(functools.partial(one_head, head))


def local_gradient(place, counts, token_keys, token_values, step_rates, fast_weights):
    heads, mats, width, _ = fast_weights.shape
    tokens = token_keys.shape[0]
    raw = pl.BlockSpec((tokens, heads, width), lambda head: (0, 0, 0))
    return pl.pallas_call(
        gradient_kernel,
        out_shape=(
            jax.ShapeDtypeStruct((heads * mats * width, width), jnp.bfloat16),
            jax.ShapeDtypeStruct((2, heads, tokens, width), jnp.bfloat16),
        ),
        grid=(heads,),
        in_specs=[
            SMEM,
            SMEM,
            raw,
            raw,
            pl.BlockSpec((heads, tokens), lambda head: (0, 0)),
            pl.BlockSpec((1, mats, width, width), lambda head: (head, 0, 0, 0)),
        ],
        out_specs=(
            pl.BlockSpec((mats * width, width), lambda head: (head, 0)),
            pl.BlockSpec((2, 1, tokens, width), lambda head: (0, head, 0, 0)),
        ),
        name="gradient",
        cost_estimate=pl.CostEstimate(
            flops=14 * 256 * width * width * heads, transcendentals=131072, bytes_accessed=3000000
        ),
    )(place, counts, token_keys, token_values, step_rates.T, fast_weights)


def window_kernel(place_ref, counts_ref, queries_ref, own_ref, near_ref, far_ref, window_ref, turned_ref):
    tokens, heads, width = queries_ref.shape
    row = lax.broadcasted_iota(jnp.int32, (tokens, tokens), 0)
    column = lax.broadcasted_iota(jnp.int32, (tokens, tokens), 1)
    blocks = (
        (own_ref, (column <= row) & (column < place_count(counts_ref, place_ref, 0))),
        (near_ref, column < place_count(counts_ref, place_ref, 1)),
        (far_ref, (column > row) & (column < place_count(counts_ref, place_ref, 2))),
    )
    scale = 1.0 / math.sqrt(width)
    for head in range(heads):
        queries = queries_ref[:, head, :]
        turned_ref[head] = queries
        scores = [
            jnp.where(allowed, product(queries, block[0, head], 1, 1) * scale, LOWEST)
            for block, allowed in blocks
        ]
        top = jnp.max(functools.reduce(jnp.maximum, scores), axis=1, keepdims=True)
        expo = [jnp.exp(score - top) for score in scores]
        mass = jnp.sum(sum(expo), axis=1, keepdims=True)
        total = sum(
            product(part.astype(jnp.bfloat16), block[1, head], 1, 0)
            for part, (block, _) in zip(expo, blocks)
        )
        window_ref[:, head * width : (head + 1) * width] = total / mass


def window_attention(place, counts, queries, own, near, far):
    tokens, heads, width = queries.shape
    return pl.pallas_call(
        window_kernel,
        out_shape=(
            jax.ShapeDtypeStruct((tokens, heads * width), jnp.float32),
            jax.ShapeDtypeStruct((heads, tokens, width), jnp.bfloat16),
        ),
        in_specs=[SMEM, SMEM] + [VMEM] * 4,
        out_specs=(VMEM, VMEM),
        name="window",
        compiler_params=pltpu.CompilerParams(vmem_limit_bytes=VMEM_BYTES),
        cost_estimate=pl.CostEstimate(
            flops=12 * tokens * tokens * width * heads,
            transcendentals=400000,
            bytes_accessed=3000000,
        ),
    )(place, counts, queries, own, near, far)


def feature_kernel(
    place_ref,
    counts_ref,
    queries_ref,
    window_ref,
    weights_ref,
    features_ref,
    held_queries,
    held_window,
    held_weights,
    sems,
):
    heads, tokens, width = held_queries.shape
    mats = 3
    fetches = []
    for head in range(heads):
        fetches.append(
            pltpu.make_async_copy(
                queries_ref.at[head], held_queries.at[head], sems.at[len(fetches)]
            )
        )
        for index in range(mats):
            rows = pl.ds((head * mats + index) * width, width)
            fetches.append(
                pltpu.make_async_copy(
                    weights_ref.at[rows], held_weights.at[rows], sems.at[len(fetches)]
                )
            )
    fetches.append(pltpu.make_async_copy(window_ref, held_window, sems.at[len(fetches)]))
    for fetch in fetches:
        fetch.start()
    valid = lax.broadcasted_iota(jnp.int32, (tokens, 1), 0) < place_count(counts_ref, place_ref, 0)
    learned = []
    for head in range(heads):
        for fetch in fetches[head * (mats + 1) : (head + 1) * (mats + 1)]:
            fetch.wait()
        queries = held_queries[head]
        first = head * mats * width
        gate = product(queries, held_weights[first : first + width, :], 1, 1)
        up = product(queries, held_weights[first + width : first + 2 * width, :], 1, 1)
        hidden = (gate * jax.nn.sigmoid(gate) * up).astype(jnp.bfloat16)
        learned.append(
            product(hidden, held_weights[first + 2 * width : first + 3 * width, :], 1, 1)
        )
    fetches[-1].wait()
    for head in range(heads):
        columns = slice(head * width, (head + 1) * width)
        features_ref[:, columns] = jnp.where(
            valid, learned[head] + held_window[:, columns], 0.0
        ).astype(jnp.bfloat16)


def features_of(place, counts, queries, window, new_flat):
    heads, tokens, width = queries.shape
    return pl.pallas_call(
        feature_kernel,
        out_shape=jax.ShapeDtypeStruct((tokens, heads * width), jnp.bfloat16),
        in_specs=[SMEM, SMEM] + [pl.BlockSpec(memory_space=pl.ANY)] * 3,
        out_specs=VMEM,
        scratch_shapes=[
            pltpu.VMEM(queries.shape, jnp.bfloat16),
            pltpu.VMEM(window.shape, jnp.float32),
            pltpu.VMEM(new_flat.shape, jnp.bfloat16),
            pltpu.SemaphoreType.DMA((4 * heads + 1,)),
        ],
        name="features",
        cost_estimate=pl.CostEstimate(
            flops=6 * tokens * width * width * heads, transcendentals=131072, bytes_accessed=2000000
        ),
    )(place, counts, queries, window, new_flat)


def split_kernel(place_ref, mine_in_ref, theirs_in_ref, mine_ref, theirs_ref):
    mine_ref[...] = mine_in_ref[...]
    theirs_ref[...] = theirs_in_ref[...]


def column_halves(head_place, out_weight):
    depth, columns = out_weight.shape
    half = columns // 2
    tile = half // 2
    piece = jax.ShapeDtypeStruct((depth, half), out_weight.dtype)
    return pl.pallas_call(
        split_kernel,
        out_shape=(piece, piece),
        grid_spec=pltpu.PrefetchScalarGridSpec(
            num_scalar_prefetch=1,
            grid=(half // tile,),
            in_specs=[
                pl.BlockSpec((depth, tile), lambda step, place: (0, place[0] * 2 + step)),
                pl.BlockSpec((depth, tile), lambda step, place: (0, (1 - place[0]) * 2 + step)),
            ],
            out_specs=(
                pl.BlockSpec((depth, tile), lambda step, place: (0, step)),
                pl.BlockSpec((depth, tile), lambda step, place: (0, step)),
            ),
        ),
        name="split",
        compiler_params=pltpu.CompilerParams(vmem_limit_bytes=VMEM_BYTES),
        cost_estimate=pl.CostEstimate(flops=0, transcendentals=0, bytes_accessed=8000000),
    )(head_place, out_weight, out_weight)


def own_project_kernel(own_ref, weight_ref, out_ref):
    out_ref[...] = jnp.dot(own_ref[...], weight_ref[...], preferred_element_type=jnp.float32)


def own_projected(own, weight):
    return pl.pallas_call(
        own_project_kernel,
        out_shape=jax.ShapeDtypeStruct((own.shape[0], weight.shape[1]), jnp.float32),
        in_specs=[VMEM, VMEM],
        out_specs=VMEM,
        name="own_project",
        compiler_params=pltpu.CompilerParams(vmem_limit_bytes=VMEM_BYTES),
        cost_estimate=pl.CostEstimate(
            flops=2 * own.shape[0] * weight.size, transcendentals=0, bytes_accessed=4000000
        ),
    )(own, weight)


def project_kernel(other_ref, weight_ref, own_ref, out_ref, held_weight, held_out, sems):
    tiles = held_out.shape[0]
    tile = held_out.shape[2]
    fetches = [
        pltpu.make_async_copy(
            weight_ref.at[:, step * tile : (step + 1) * tile], held_weight.at[step], sems.at[0, step]
        )
        for step in range(tiles)
    ]
    for fetch in fetches:
        fetch.start()
    stores = []
    for step in range(tiles):
        columns = slice(step * tile, (step + 1) * tile)
        fetches[step].wait()
        held_out[step] = (
            own_ref[:, columns]
            + jnp.dot(other_ref[...], held_weight[step], preferred_element_type=jnp.float32)
        ).astype(jnp.bfloat16)
        stores.append(
            pltpu.make_async_copy(held_out.at[step], out_ref.at[:, columns], sems.at[1, step])
        )
        stores[step].start()
    for store in stores:
        store.wait()


def projected(other, weight, own_product):
    tokens, depth = other.shape
    columns = weight.shape[1]
    tiles = 4
    tile = columns // tiles
    return pl.pallas_call(
        project_kernel,
        out_shape=jax.ShapeDtypeStruct((tokens, columns), jnp.bfloat16),
        in_specs=[VMEM, pl.BlockSpec(memory_space=pl.ANY), VMEM],
        out_specs=pl.BlockSpec(memory_space=pl.ANY),
        scratch_shapes=[
            pltpu.VMEM((tiles, depth, tile), jnp.bfloat16),
            pltpu.VMEM((tiles, tokens, tile), jnp.bfloat16),
            pltpu.SemaphoreType.DMA((2, tiles)),
        ],
        name="project",
        compiler_params=pltpu.CompilerParams(vmem_limit_bytes=VMEM_BYTES),
        cost_estimate=pl.CostEstimate(
            flops=2 * tokens * depth * columns, transcendentals=0, bytes_accessed=6000000
        ),
    )(other, weight, own_product)


def collect_kernel(blocks_ref, sums_ref):
    total = jnp.sum(blocks_ref[...].astype(jnp.float32), axis=0)
    sums_ref[...] = jnp.broadcast_to(total[None], sums_ref.shape)


def collected(copies, blocks):
    return pl.pallas_call(
        collect_kernel,
        out_shape=jax.ShapeDtypeStruct((copies, *blocks.shape[1:]), jnp.float32),
        in_specs=[VMEM],
        out_specs=VMEM,
        name="collect",
        compiler_params=pltpu.CompilerParams(vmem_limit_bytes=VMEM_BYTES),
        cost_estimate=pl.CostEstimate(flops=400000, transcendentals=0, bytes_accessed=800000),
    )(blocks)


def refresh_kernel(total, sums_ref, old_ref, rows_ref):
    gradient = jnp.sum(sums_ref[...], axis=0)
    old = old_ref[...]
    updated = old - gradient / math.sqrt(total)
    old_norm = jnp.sqrt(jnp.sum(old * old, axis=1, keepdims=True))
    fresh = updated * old_norm / jnp.sqrt(jnp.sum(updated * updated, axis=1, keepdims=True) + 1e-06)
    rows_ref[...] = jnp.broadcast_to(fresh.astype(jnp.bfloat16)[None], rows_ref.shape)


def refreshed(total, copies, sums, old_rows):
    return pl.pallas_call(
        functools.partial(refresh_kernel, total),
        out_shape=jax.ShapeDtypeStruct((copies, *old_rows.shape), jnp.bfloat16),
        in_specs=[VMEM, VMEM],
        out_specs=VMEM,
        name="refresh",
        compiler_params=pltpu.CompilerParams(vmem_limit_bytes=VMEM_BYTES),
        cost_estimate=pl.CostEstimate(flops=100000, transcendentals=0, bytes_accessed=1000000),
    )(sums, old_rows)


def shards(queries, token_keys, token_values, step_rates, counts, fast_weights, out_weight):
    tok_rows, _, head_width = queries.shape
    device_count, plane_count = lax.axis_size(CTX), lax.axis_size("p")
    plane_place, head_place = lax.axis_index("p"), lax.axis_index("head")
    place = lax.axis_index(CTX).reshape(1).astype(jnp.int32)
    local_grad, pairs = local_gradient(
        place, counts, token_keys, token_values, step_rates, fast_weights
    )
    near = passed_along(pairs, 1)
    blocks = lax.all_to_all(local_grad.reshape(plane_count, -1, head_width), "p", 0, 0, tiled=True)
    out_own, out_theirs = column_halves(
        head_place.reshape(1).astype(jnp.int32), out_weight
    )
    out_other = lax.ppermute(out_theirs, "head", [(0, 1), (1, 0)])
    sums = collected(RING, blocks)
    sums = lax.all_to_all(sums, "z", 0, 0, tiled=True)
    far = passed_along(near, 1)
    old_flat = fast_weights.reshape(-1, head_width)
    own_rows = old_flat.shape[0] // plane_count
    old_rows = lax.dynamic_slice_in_dim(old_flat, plane_place * own_rows, own_rows, 0)
    new_rows = refreshed(tok_rows * device_count, plane_count, sums, old_rows)
    new_flat = lax.all_to_all(new_rows, "p", 0, 0, tiled=True).reshape(-1, head_width)
    window, turned_queries = window_attention(place, counts, queries, pairs, near, far)
    features = features_of(place, counts, turned_queries, window, new_flat)
    other = lax.ppermute(features, "head", [(0, 1), (1, 0)])
    own_product = own_projected(features, out_own)
    return projected(other, out_other, own_product)


def solution(mesh):
    fine = Mesh(mesh.devices.reshape(RING, -1, 2), ("z", "p", "head"))
    in_specs = (
        P(CTX, "head", None),
        P(CTX, "head", None),
        P(CTX, "head", None),
        P(CTX, "head"),
        P(),
        P("head", None, None, None),
        P("head", None),
    )
    return jax.shard_map(
        shards, mesh=fine, in_specs=in_specs, out_specs=P(CTX, "head"), check_vma=False
    )
```

```python
import functools
import math

import jax
import jax.numpy as jnp
from jax import lax
from jax.experimental import pallas as pl
from jax.experimental.pallas import tpu as pltpu
from jax.sharding import Mesh, PartitionSpec as P


RING = 4
CTX = ("z", "p")
VMEM = pl.BlockSpec(memory_space=pltpu.VMEM)
SMEM = pl.BlockSpec(memory_space=pltpu.SMEM)
LOWEST = -1e30
VMEM_BYTES = 24 << 20


def passed_along(value, steps):
    count = lax.axis_size(CTX)
    return lax.ppermute(value, CTX, [(source, source + steps) for source in range(count - steps)])


def turned(value, steps):
    return lax.ppermute(value, "z", [(place, (place + steps) % RING) for place in range(RING)])


def product(left, right, left_dim, right_dim):
    return lax.dot_general(
        left,
        right,
        (((left_dim,), (right_dim,)), ((), ())),
        preferred_element_type=jnp.float32,
    )


def place_count(counts_ref, place_ref, back_step):
    place = place_ref[0] - back_step
    return jnp.where(place >= 0, counts_ref[jnp.maximum(place, 0)], 0)


def gradient_kernel(
    place_ref, counts_ref, keys_ref, values_ref, rates_ref, weights_ref, grad_ref, pairs_ref
):
    tokens, heads, width = keys_ref.shape

    def one_head(head):
        valid = lax.broadcasted_iota(jnp.int32, (tokens, 1), 0) < place_count(
            counts_ref, place_ref, 0
        )
        rates_all = jnp.concatenate(
            [rates_ref[...], jnp.zeros((8 - heads, tokens), jnp.float32)], 0
        ).T
        keys, values = keys_ref[:, head, :], values_ref[:, head, :]
        pairs_ref[0, 0] = keys
        pairs_ref[1, 0] = values
        rates = jnp.where(valid, rates_all[:, head : head + 1], 0.0)
        scaled = (rates * values.astype(jnp.float32)).astype(jnp.bfloat16)
        gate_weight = weights_ref[0, 0].astype(jnp.bfloat16)
        up_weight = weights_ref[0, 1].astype(jnp.bfloat16)
        down_weight = weights_ref[0, 2].astype(jnp.bfloat16)
        gate_pre = product(keys, gate_weight, 1, 1)
        up_pre = product(keys, up_weight, 1, 1)
        back = -product(scaled, down_weight, 1, 0)
        sigmoid = jax.nn.sigmoid(gate_pre)
        gate_act = gate_pre * sigmoid
        hidden = (gate_act * up_pre).astype(jnp.bfloat16)
        slope = sigmoid * (1.0 + gate_pre * (1.0 - sigmoid))
        grad_gate = (back * up_pre * slope).astype(jnp.bfloat16)
        grad_up = (back * gate_act).astype(jnp.bfloat16)
        mats = (
            product(grad_gate, keys, 0, 0),
            product(grad_up, keys, 0, 0),
            -product(scaled, hidden, 0, 0),
        )
        for index, mat in enumerate(mats):
            grad_ref[index * width : (index + 1) * width, :] = mat.astype(jnp.bfloat16)

    for head in range(heads):
        pl.when(pl.program_id(0) == head)(functools.partial(one_head, head))


def local_gradient(place, counts, token_keys, token_values, step_rates, fast_weights):
    heads, mats, width, _ = fast_weights.shape
    tokens = token_keys.shape[0]
    raw = pl.BlockSpec((tokens, heads, width), lambda head: (0, 0, 0))
    return pl.pallas_call(
        gradient_kernel,
        out_shape=(
            jax.ShapeDtypeStruct((heads * mats * width, width), jnp.bfloat16),
            jax.ShapeDtypeStruct((2, heads, tokens, width), jnp.bfloat16),
        ),
        grid=(heads,),
        in_specs=[
            SMEM,
            SMEM,
            raw,
            raw,
            pl.BlockSpec((heads, tokens), lambda head: (0, 0)),
            pl.BlockSpec((1, mats, width, width), lambda head: (head, 0, 0, 0)),
        ],
        out_specs=(
            pl.BlockSpec((mats * width, width), lambda head: (head, 0)),
            pl.BlockSpec((2, 1, tokens, width), lambda head: (0, head, 0, 0)),
        ),
        name="gradient",
        cost_estimate=pl.CostEstimate(
            flops=14 * 256 * width * width * heads, transcendentals=131072, bytes_accessed=3000000
        ),
    )(place, counts, token_keys, token_values, step_rates.T, fast_weights)


def window_kernel(place_ref, counts_ref, queries_ref, own_ref, near_ref, far_ref, window_ref, turned_ref):
    tokens, heads, width = queries_ref.shape
    row = lax.broadcasted_iota(jnp.int32, (tokens, tokens), 0)
    column = lax.broadcasted_iota(jnp.int32, (tokens, tokens), 1)
    blocks = (
        (own_ref, (column <= row) & (column < place_count(counts_ref, place_ref, 0))),
        (near_ref, column < place_count(counts_ref, place_ref, 1)),
        (far_ref, (column > row) & (column < place_count(counts_ref, place_ref, 2))),
    )
    scale = 1.0 / math.sqrt(width)
    for head in range(heads):
        queries = queries_ref[:, head, :]
        turned_ref[head] = queries
        scores = [
            jnp.where(allowed, product(queries, block[0, head], 1, 1) * scale, LOWEST)
            for block, allowed in blocks
        ]
        top = jnp.max(functools.reduce(jnp.maximum, scores), axis=1, keepdims=True)
        expo = [jnp.exp(score - top) for score in scores]
        mass = jnp.sum(sum(expo), axis=1, keepdims=True)
        total = sum(
            product(part.astype(jnp.bfloat16), block[1, head], 1, 0)
            for part, (block, _) in zip(expo, blocks)
        )
        window_ref[:, head * width : (head + 1) * width] = total / mass


def window_attention(place, counts, queries, own, near, far):
    tokens, heads, width = queries.shape
    return pl.pallas_call(
        window_kernel,
        out_shape=(
            jax.ShapeDtypeStruct((tokens, heads * width), jnp.float32),
            jax.ShapeDtypeStruct((heads, tokens, width), jnp.bfloat16),
        ),
        in_specs=[SMEM, SMEM] + [VMEM] * 4,
        out_specs=(VMEM, VMEM),
        name="window",
        compiler_params=pltpu.CompilerParams(vmem_limit_bytes=VMEM_BYTES),
        cost_estimate=pl.CostEstimate(
            flops=12 * tokens * tokens * width * heads,
            transcendentals=400000,
            bytes_accessed=3000000,
        ),
    )(place, counts, queries, own, near, far)


def feature_kernel(place_ref, counts_ref, queries_ref, window_ref, weights_ref, features_ref):
    heads, tokens, width = queries_ref.shape
    valid = lax.broadcasted_iota(jnp.int32, (tokens, 1), 0) < place_count(counts_ref, place_ref, 0)
    for head in range(heads):
        queries = queries_ref[head]
        first = head * 3 * width
        gate = product(queries, weights_ref[first : first + width, :], 1, 1)
        up = product(queries, weights_ref[first + width : first + 2 * width, :], 1, 1)
        hidden = (gate * jax.nn.sigmoid(gate) * up).astype(jnp.bfloat16)
        learned = product(hidden, weights_ref[first + 2 * width : first + 3 * width, :], 1, 1)
        columns = slice(head * width, (head + 1) * width)
        features_ref[:, columns] = jnp.where(
            valid, learned + window_ref[:, columns], 0.0
        ).astype(jnp.bfloat16)


def features_of(place, counts, queries, window, new_flat):
    heads, tokens, width = queries.shape
    return pl.pallas_call(
        feature_kernel,
        out_shape=jax.ShapeDtypeStruct((tokens, heads * width), jnp.bfloat16),
        in_specs=[SMEM, SMEM] + [VMEM] * 3,
        out_specs=VMEM,
        name="features",
        compiler_params=pltpu.CompilerParams(vmem_limit_bytes=VMEM_BYTES),
        cost_estimate=pl.CostEstimate(
            flops=6 * tokens * width * width * heads, transcendentals=131072, bytes_accessed=2000000
        ),
    )(place, counts, queries, window, new_flat)


def split_kernel(place_ref, mine_in_ref, theirs_in_ref, mine_ref, theirs_ref):
    mine_ref[...] = mine_in_ref[...]
    theirs_ref[...] = theirs_in_ref[...]


def column_halves(head_place, out_weight):
    depth, columns = out_weight.shape
    half = columns // 2
    tile = half // 2
    piece = jax.ShapeDtypeStruct((depth, half), out_weight.dtype)
    return pl.pallas_call(
        split_kernel,
        out_shape=(piece, piece),
        grid_spec=pltpu.PrefetchScalarGridSpec(
            num_scalar_prefetch=1,
            grid=(half // tile,),
            in_specs=[
                pl.BlockSpec((depth, tile), lambda step, place: (0, place[0] * 2 + step)),
                pl.BlockSpec((depth, tile), lambda step, place: (0, (1 - place[0]) * 2 + step)),
            ],
            out_specs=(
                pl.BlockSpec((depth, tile), lambda step, place: (0, step)),
                pl.BlockSpec((depth, tile), lambda step, place: (0, step)),
            ),
        ),
        name="split",
        cost_estimate=pl.CostEstimate(flops=0, transcendentals=0, bytes_accessed=8000000),
    )(head_place, out_weight, out_weight)


def own_project_kernel(own_ref, weight_ref, out_ref, held_weight, sems):
    tiles, _, tile = held_weight.shape
    fetches = [
        pltpu.make_async_copy(
            weight_ref.at[:, step * tile : (step + 1) * tile], held_weight.at[step], sems.at[step]
        )
        for step in range(tiles)
    ]
    for fetch in fetches:
        fetch.start()
    for step in range(tiles):
        fetches[step].wait()
        out_ref[:, step * tile : (step + 1) * tile] = jnp.dot(
            own_ref[...], held_weight[step], preferred_element_type=jnp.float32
        )


def own_projected(own, weight):
    depth, columns = weight.shape
    tiles = 4
    return pl.pallas_call(
        own_project_kernel,
        out_shape=jax.ShapeDtypeStruct((own.shape[0], columns), jnp.float32),
        in_specs=[VMEM, pl.BlockSpec(memory_space=pl.ANY)],
        out_specs=VMEM,
        scratch_shapes=[
            pltpu.VMEM((tiles, depth, columns // tiles), jnp.bfloat16),
            pltpu.SemaphoreType.DMA((tiles,)),
        ],
        name="own_project",
        compiler_params=pltpu.CompilerParams(vmem_limit_bytes=VMEM_BYTES),
        cost_estimate=pl.CostEstimate(
            flops=2 * own.shape[0] * weight.size, transcendentals=0, bytes_accessed=4000000
        ),
    )(own, weight)


def project_kernel(other_ref, weight_ref, own_ref, out_ref, held_weight, held_out, sems):
    tiles = held_out.shape[0]
    tile = held_out.shape[2]
    fetches = [
        pltpu.make_async_copy(
            weight_ref.at[:, step * tile : (step + 1) * tile], held_weight.at[step], sems.at[0, step]
        )
        for step in range(tiles)
    ]
    for fetch in fetches:
        fetch.start()
    stores = []
    for step in range(tiles):
        columns = slice(step * tile, (step + 1) * tile)
        fetches[step].wait()
        held_out[step] = (
            own_ref[:, columns]
            + jnp.dot(other_ref[...], held_weight[step], preferred_element_type=jnp.float32)
        ).astype(jnp.bfloat16)
        stores.append(
            pltpu.make_async_copy(held_out.at[step], out_ref.at[:, columns], sems.at[1, step])
        )
        stores[step].start()
    for store in stores:
        store.wait()


def projected(other, weight, own_product):
    tokens, depth = other.shape
    columns = weight.shape[1]
    tiles = 4
    tile = columns // tiles
    return pl.pallas_call(
        project_kernel,
        out_shape=jax.ShapeDtypeStruct((tokens, columns), jnp.bfloat16),
        in_specs=[VMEM, pl.BlockSpec(memory_space=pl.ANY), VMEM],
        out_specs=pl.BlockSpec(memory_space=pl.ANY),
        scratch_shapes=[
            pltpu.VMEM((tiles, depth, tile), jnp.bfloat16),
            pltpu.VMEM((tiles, tokens, tile), jnp.bfloat16),
            pltpu.SemaphoreType.DMA((2, tiles)),
        ],
        name="project",
        compiler_params=pltpu.CompilerParams(vmem_limit_bytes=VMEM_BYTES),
        cost_estimate=pl.CostEstimate(
            flops=2 * tokens * depth * columns, transcendentals=0, bytes_accessed=6000000
        ),
    )(other, weight, own_product)


def collect_kernel(blocks_ref, sums_ref):
    sums_ref[...] = jnp.sum(blocks_ref[...].astype(jnp.float32), axis=0)


def collected(blocks):
    return pl.pallas_call(
        collect_kernel,
        out_shape=jax.ShapeDtypeStruct(blocks.shape[1:], jnp.float32),
        in_specs=[VMEM],
        out_specs=VMEM,
        name="collect",
        compiler_params=pltpu.CompilerParams(vmem_limit_bytes=VMEM_BYTES),
        cost_estimate=pl.CostEstimate(flops=400000, transcendentals=0, bytes_accessed=800000),
    )(blocks)


def refresh_kernel(total, own_ref, behind_ref, opposite_ref, ahead_ref, old_ref, rows_ref):
    gradient = (own_ref[...] + opposite_ref[...]) + (behind_ref[...] + ahead_ref[...])
    old = old_ref[...]
    updated = old - gradient / math.sqrt(total)
    old_norm = jnp.sqrt(jnp.sum(old * old, axis=1, keepdims=True))
    fresh = updated * old_norm / jnp.sqrt(jnp.sum(updated * updated, axis=1, keepdims=True) + 1e-06)
    rows_ref[...] = jnp.broadcast_to(fresh.astype(jnp.bfloat16)[None], rows_ref.shape)


def refreshed(total, copies, parts, old_rows):
    return pl.pallas_call(
        functools.partial(refresh_kernel, total),
        out_shape=jax.ShapeDtypeStruct((copies, *old_rows.shape), jnp.bfloat16),
        in_specs=[VMEM] * (RING + 1),
        out_specs=VMEM,
        name="refresh",
        compiler_params=pltpu.CompilerParams(vmem_limit_bytes=VMEM_BYTES),
        cost_estimate=pl.CostEstimate(flops=100000, transcendentals=0, bytes_accessed=1000000),
    )(*parts, old_rows)


def shards(queries, token_keys, token_values, step_rates, counts, fast_weights, out_weight):
    tok_rows, _, head_width = queries.shape
    device_count, plane_count = lax.axis_size(CTX), lax.axis_size("p")
    plane_place, head_place = lax.axis_index("p"), lax.axis_index("head")
    place = lax.axis_index(CTX).reshape(1).astype(jnp.int32)
    local_grad, pairs = local_gradient(
        place, counts, token_keys, token_values, step_rates, fast_weights
    )
    near = passed_along(pairs, 1)
    blocks = lax.all_to_all(local_grad.reshape(plane_count, -1, head_width), "p", 0, 0, tiled=True)
    out_own, out_theirs = column_halves(
        head_place.reshape(1).astype(jnp.int32), out_weight
    )
    out_other = lax.ppermute(out_theirs, "head", [(0, 1), (1, 0)])
    parts = [collected(blocks)]
    for steps in range(1, RING):
        parts.append(turned(parts[0], steps))
    far = passed_along(near, 1)
    old_flat = fast_weights.reshape(-1, head_width)
    own_rows = old_flat.shape[0] // plane_count
    old_rows = lax.dynamic_slice_in_dim(old_flat, plane_place * own_rows, own_rows, 0)
    new_rows = refreshed(tok_rows * device_count, plane_count, parts, old_rows)
    new_flat = lax.all_to_all(new_rows, "p", 0, 0, tiled=True).reshape(-1, head_width)
    window, turned_queries = window_attention(place, counts, queries, pairs, near, far)
    features = features_of(place, counts, turned_queries, window, new_flat)
    other = lax.ppermute(features, "head", [(0, 1), (1, 0)])
    own_product = own_projected(
        features, pltpu.with_memory_space_constraint(out_own, pltpu.MemorySpace.HBM)
    )
    return projected(
        other, pltpu.with_memory_space_constraint(out_other, pltpu.MemorySpace.HBM), own_product
    )


def solution(mesh):
    fine = Mesh(mesh.devices.reshape(RING, -1, 2), ("z", "p", "head"))
    in_specs = (
        P(CTX, "head", None),
        P(CTX, "head", None),
        P(CTX, "head", None),
        P(CTX, "head"),
        P(),
        P("head", None, None, None),
        P("head", None),
    )
    return jax.shard_map(
        shards, mesh=fine, in_specs=in_specs, out_specs=P(CTX, "head"), check_vma=False
    )
```

```python
import functools
import math

import jax
import jax.numpy as jnp
from jax import lax
from jax.experimental import pallas as pl
from jax.experimental.pallas import tpu as pltpu
from jax.sharding import Mesh, PartitionSpec as P


RING = 4
TILES = 4
CTX = ("z", "p")
VMEM = pl.BlockSpec(memory_space=pltpu.VMEM)
SMEM = pl.BlockSpec(memory_space=pltpu.SMEM)
LOWEST = -1e30
VMEM_BYTES = 24 << 20


def passed_along(value, steps):
    count = lax.axis_size(CTX)
    return lax.ppermute(value, CTX, [(source, source + steps) for source in range(count - steps)])


def product(left, right, left_dim, right_dim):
    return lax.dot_general(
        left,
        right,
        (((left_dim,), (right_dim,)), ((), ())),
        preferred_element_type=jnp.float32,
    )


def place_count(counts_ref, place_ref, back_step):
    place = place_ref[0] - back_step
    return jnp.where(place >= 0, counts_ref[jnp.maximum(place, 0)], 0)


def gradient_kernel(
    place_ref, counts_ref, keys_ref, values_ref, rates_ref, weights_ref, grad_ref, pairs_ref
):
    tokens, heads, width = keys_ref.shape

    def one_head(head):
        valid = lax.broadcasted_iota(jnp.int32, (tokens, 1), 0) < place_count(
            counts_ref, place_ref, 0
        )
        rates_all = jnp.concatenate(
            [rates_ref[...], jnp.zeros((8 - heads, tokens), jnp.float32)], 0
        ).T
        keys, values = keys_ref[:, head, :], values_ref[:, head, :]
        pairs_ref[0, 0] = keys
        pairs_ref[1, 0] = values
        rates = jnp.where(valid, rates_all[:, head : head + 1], 0.0)
        scaled = (rates * values.astype(jnp.float32)).astype(jnp.bfloat16)
        gate_weight = weights_ref[0, 0].astype(jnp.bfloat16)
        up_weight = weights_ref[0, 1].astype(jnp.bfloat16)
        down_weight = weights_ref[0, 2].astype(jnp.bfloat16)
        gate_pre = product(keys, gate_weight, 1, 1)
        up_pre = product(keys, up_weight, 1, 1)
        back = -product(scaled, down_weight, 1, 0)
        sigmoid = jax.nn.sigmoid(gate_pre)
        gate_act = gate_pre * sigmoid
        hidden = (gate_act * up_pre).astype(jnp.bfloat16)
        slope = sigmoid * (1.0 + gate_pre * (1.0 - sigmoid))
        grad_gate = (back * up_pre * slope).astype(jnp.bfloat16)
        grad_up = (back * gate_act).astype(jnp.bfloat16)
        mats = (
            product(grad_gate, keys, 0, 0),
            product(grad_up, keys, 0, 0),
            -product(scaled, hidden, 0, 0),
        )
        for index, mat in enumerate(mats):
            grad_ref[index * width : (index + 1) * width, :] = mat.astype(jnp.bfloat16)

    for head in range(heads):
        pl.when(pl.program_id(0) == head)(functools.partial(one_head, head))


def local_gradient(place, counts, token_keys, token_values, step_rates, fast_weights):
    heads, mats, width, _ = fast_weights.shape
    tokens = token_keys.shape[0]
    raw = pl.BlockSpec((tokens, heads, width), lambda head: (0, 0, 0))
    return pl.pallas_call(
        gradient_kernel,
        out_shape=(
            jax.ShapeDtypeStruct((heads * mats * width, width), jnp.bfloat16),
            jax.ShapeDtypeStruct((2, heads, tokens, width), jnp.bfloat16),
        ),
        grid=(heads,),
        in_specs=[
            SMEM,
            SMEM,
            raw,
            raw,
            pl.BlockSpec((heads, tokens), lambda head: (0, 0)),
            pl.BlockSpec((1, mats, width, width), lambda head: (head, 0, 0, 0)),
        ],
        out_specs=(
            pl.BlockSpec((mats * width, width), lambda head: (head, 0)),
            pl.BlockSpec((2, 1, tokens, width), lambda head: (0, head, 0, 0)),
        ),
        name="gradient",
        cost_estimate=pl.CostEstimate(
            flops=14 * 256 * width * width * heads, transcendentals=131072, bytes_accessed=3000000
        ),
    )(place, counts, token_keys, token_values, step_rates.T, fast_weights)


def window_kernel(place_ref, counts_ref, queries_ref, own_ref, near_ref, far_ref, window_ref, turned_ref):
    tokens, heads, width = queries_ref.shape
    row = lax.broadcasted_iota(jnp.int32, (tokens, tokens), 0)
    column = lax.broadcasted_iota(jnp.int32, (tokens, tokens), 1)
    blocks = (
        (own_ref, (column <= row) & (column < place_count(counts_ref, place_ref, 0))),
        (near_ref, column < place_count(counts_ref, place_ref, 1)),
        (far_ref, (column > row) & (column < place_count(counts_ref, place_ref, 2))),
    )
    scale = 1.0 / math.sqrt(width)
    for head in range(heads):
        queries = queries_ref[:, head, :]
        turned_ref[head] = queries
        scores = [
            jnp.where(allowed, product(queries, block[0, head], 1, 1) * scale, LOWEST)
            for block, allowed in blocks
        ]
        top = jnp.max(functools.reduce(jnp.maximum, scores), axis=1, keepdims=True)
        expo = [jnp.exp(score - top) for score in scores]
        mass = jnp.sum(sum(expo), axis=1, keepdims=True)
        total = sum(
            product(part.astype(jnp.bfloat16), block[1, head], 1, 0)
            for part, (block, _) in zip(expo, blocks)
        )
        window_ref[:, head * width : (head + 1) * width] = total / mass


def window_attention(place, counts, queries, own, near, far):
    tokens, heads, width = queries.shape
    return pl.pallas_call(
        window_kernel,
        out_shape=(
            jax.ShapeDtypeStruct((tokens, heads * width), jnp.float32),
            jax.ShapeDtypeStruct((heads, tokens, width), jnp.bfloat16),
        ),
        in_specs=[SMEM, SMEM] + [VMEM] * 4,
        out_specs=(VMEM, VMEM),
        name="window",
        compiler_params=pltpu.CompilerParams(vmem_limit_bytes=VMEM_BYTES),
        cost_estimate=pl.CostEstimate(
            flops=12 * tokens * tokens * width * heads,
            transcendentals=400000,
            bytes_accessed=3000000,
        ),
    )(place, counts, queries, own, near, far)


def feature_kernel(place_ref, counts_ref, queries_ref, window_ref, weights_ref, features_ref):
    heads, tokens, width = queries_ref.shape
    valid = lax.broadcasted_iota(jnp.int32, (tokens, 1), 0) < place_count(counts_ref, place_ref, 0)
    for head in range(heads):
        queries = queries_ref[head]
        first = head * 3 * width
        gate = product(queries, weights_ref[first : first + width, :], 1, 1)
        up = product(queries, weights_ref[first + width : first + 2 * width, :], 1, 1)
        hidden = (gate * jax.nn.sigmoid(gate) * up).astype(jnp.bfloat16)
        learned = product(hidden, weights_ref[first + 2 * width : first + 3 * width, :], 1, 1)
        columns = slice(head * width, (head + 1) * width)
        features_ref[:, columns] = jnp.where(
            valid, learned + window_ref[:, columns], 0.0
        ).astype(jnp.bfloat16)


def features_of(place, counts, queries, window, new_flat):
    heads, tokens, width = queries.shape
    return pl.pallas_call(
        feature_kernel,
        out_shape=jax.ShapeDtypeStruct((tokens, heads * width), jnp.bfloat16),
        in_specs=[SMEM, SMEM] + [VMEM] * 3,
        out_specs=VMEM,
        name="features",
        compiler_params=pltpu.CompilerParams(vmem_limit_bytes=VMEM_BYTES),
        cost_estimate=pl.CostEstimate(
            flops=6 * tokens * width * width * heads, transcendentals=131072, bytes_accessed=2000000
        ),
    )(place, counts, queries, window, new_flat)


def split_kernel(place_ref, mine_in_ref, theirs_in_ref, mine_ref, theirs_ref):
    mine_ref[0] = mine_in_ref[...]
    theirs_ref[0] = theirs_in_ref[...]


def column_halves(head_place, out_weight):
    depth, columns = out_weight.shape
    tile = columns // 2 // TILES
    piece = jax.ShapeDtypeStruct((TILES, depth, tile), out_weight.dtype)
    out_spec = pl.BlockSpec((1, depth, tile), lambda step, place: (step, 0, 0))
    return pl.pallas_call(
        split_kernel,
        out_shape=(piece, piece),
        grid_spec=pltpu.PrefetchScalarGridSpec(
            num_scalar_prefetch=1,
            grid=(TILES,),
            in_specs=[
                pl.BlockSpec((depth, tile), lambda step, place: (0, place[0] * TILES + step)),
                pl.BlockSpec((depth, tile), lambda step, place: (0, (1 - place[0]) * TILES + step)),
            ],
            out_specs=(out_spec, out_spec),
        ),
        name="split",
        cost_estimate=pl.CostEstimate(flops=0, transcendentals=0, bytes_accessed=8000000),
    )(head_place, out_weight, out_weight)


def own_project_kernel(own_ref, weight_ref, out_ref, held_weight, sems):
    fetches = [
        pltpu.make_async_copy(weight_ref.at[step], held_weight.at[step], sems.at[step])
        for step in range(TILES)
    ]
    for fetch in fetches:
        fetch.start()
    tile = held_weight.shape[2]
    for step in range(TILES):
        fetches[step].wait()
        out_ref[:, step * tile : (step + 1) * tile] = jnp.dot(
            own_ref[...], held_weight[step], preferred_element_type=jnp.float32
        )


def own_projected(own, weight):
    return pl.pallas_call(
        own_project_kernel,
        out_shape=jax.ShapeDtypeStruct((own.shape[0], TILES * weight.shape[2]), jnp.float32),
        in_specs=[VMEM, pl.BlockSpec(memory_space=pl.ANY)],
        out_specs=VMEM,
        scratch_shapes=[pltpu.VMEM(weight.shape, jnp.bfloat16), pltpu.SemaphoreType.DMA((TILES,))],
        name="own_project",
        compiler_params=pltpu.CompilerParams(vmem_limit_bytes=VMEM_BYTES),
        cost_estimate=pl.CostEstimate(
            flops=2 * own.shape[0] * weight.size, transcendentals=0, bytes_accessed=4000000
        ),
    )(own, weight)


def project_kernel(other_ref, weight_ref, own_ref, out_ref, held_weight, held_out, sems):
    fetches = [
        pltpu.make_async_copy(weight_ref.at[step], held_weight.at[step], sems.at[0, step])
        for step in range(TILES)
    ]
    for fetch in fetches:
        fetch.start()
    tile = held_weight.shape[2]
    stores = []
    for step in range(TILES):
        columns = slice(step * tile, (step + 1) * tile)
        fetches[step].wait()
        held_out[step] = (
            own_ref[:, columns]
            + jnp.dot(other_ref[...], held_weight[step], preferred_element_type=jnp.float32)
        ).astype(jnp.bfloat16)
        stores.append(
            pltpu.make_async_copy(held_out.at[step], out_ref.at[:, columns], sems.at[1, step])
        )
        stores[step].start()
    for store in stores:
        store.wait()


def projected(other, weight, own_product):
    tokens = other.shape[0]
    tile = weight.shape[2]
    return pl.pallas_call(
        project_kernel,
        out_shape=jax.ShapeDtypeStruct((tokens, TILES * tile), jnp.bfloat16),
        in_specs=[VMEM, pl.BlockSpec(memory_space=pl.ANY), VMEM],
        out_specs=pl.BlockSpec(memory_space=pl.ANY),
        scratch_shapes=[
            pltpu.VMEM(weight.shape, jnp.bfloat16),
            pltpu.VMEM((TILES, tokens, tile), jnp.bfloat16),
            pltpu.SemaphoreType.DMA((2, TILES)),
        ],
        name="project",
        compiler_params=pltpu.CompilerParams(vmem_limit_bytes=VMEM_BYTES),
        cost_estimate=pl.CostEstimate(
            flops=2 * tokens * weight.size, transcendentals=0, bytes_accessed=6000000
        ),
    )(other, weight, own_product)


def collect_kernel(blocks_ref, sums_ref):
    total = jnp.sum(blocks_ref[...].astype(jnp.float32), axis=0)
    sums_ref[...] = jnp.broadcast_to(total[None], sums_ref.shape)


def collected(copies, blocks):
    return pl.pallas_call(
        collect_kernel,
        out_shape=jax.ShapeDtypeStruct((copies, *blocks.shape[1:]), jnp.float32),
        in_specs=[VMEM],
        out_specs=VMEM,
        name="collect",
        compiler_params=pltpu.CompilerParams(vmem_limit_bytes=VMEM_BYTES),
        cost_estimate=pl.CostEstimate(flops=400000, transcendentals=0, bytes_accessed=800000),
    )(blocks)


def refresh_kernel(total, sums_ref, old_ref, rows_ref):
    gradient = jnp.sum(sums_ref[...], axis=0)
    old = old_ref[...]
    updated = old - gradient / math.sqrt(total)
    old_norm = jnp.sqrt(jnp.sum(old * old, axis=1, keepdims=True))
    fresh = updated * old_norm / jnp.sqrt(jnp.sum(updated * updated, axis=1, keepdims=True) + 1e-06)
    rows_ref[...] = jnp.broadcast_to(fresh.astype(jnp.bfloat16)[None], rows_ref.shape)


def refreshed(total, copies, sums, old_rows):
    return pl.pallas_call(
        functools.partial(refresh_kernel, total),
        out_shape=jax.ShapeDtypeStruct((copies, *old_rows.shape), jnp.bfloat16),
        in_specs=[VMEM, VMEM],
        out_specs=VMEM,
        name="refresh",
        compiler_params=pltpu.CompilerParams(vmem_limit_bytes=VMEM_BYTES),
        cost_estimate=pl.CostEstimate(flops=100000, transcendentals=0, bytes_accessed=1000000),
    )(sums, old_rows)


def shards(queries, token_keys, token_values, step_rates, counts, fast_weights, out_weight):
    tok_rows, _, head_width = queries.shape
    device_count, plane_count = lax.axis_size(CTX), lax.axis_size("p")
    plane_place, head_place = lax.axis_index("p"), lax.axis_index("head")
    place = lax.axis_index(CTX).reshape(1).astype(jnp.int32)
    local_grad, pairs = local_gradient(
        place, counts, token_keys, token_values, step_rates, fast_weights
    )
    near = passed_along(pairs, 1)
    blocks = lax.all_to_all(local_grad.reshape(plane_count, -1, head_width), "p", 0, 0, tiled=True)
    out_own, out_theirs = column_halves(
        head_place.reshape(1).astype(jnp.int32), out_weight
    )
    out_other = lax.ppermute(out_theirs, "head", [(0, 1), (1, 0)])
    sums = collected(RING, blocks)
    sums = lax.all_to_all(sums, "z", 0, 0, tiled=True)
    far = passed_along(near, 1)
    old_flat = fast_weights.reshape(-1, head_width)
    own_rows = old_flat.shape[0] // plane_count
    old_rows = lax.dynamic_slice_in_dim(old_flat, plane_place * own_rows, own_rows, 0)
    new_rows = refreshed(tok_rows * device_count, plane_count, sums, old_rows)
    new_flat = lax.all_to_all(new_rows, "p", 0, 0, tiled=True).reshape(-1, head_width)
    window, turned_queries = window_attention(place, counts, queries, pairs, near, far)
    features = features_of(place, counts, turned_queries, window, new_flat)
    other = lax.ppermute(features, "head", [(0, 1), (1, 0)])
    own_product = own_projected(
        features, pltpu.with_memory_space_constraint(out_own, pltpu.MemorySpace.HBM)
    )
    return projected(
        other, pltpu.with_memory_space_constraint(out_other, pltpu.MemorySpace.HBM), own_product
    )


def solution(mesh):
    fine = Mesh(mesh.devices.reshape(RING, -1, 2), ("z", "p", "head"))
    in_specs = (
        P(CTX, "head", None),
        P(CTX, "head", None),
        P(CTX, "head", None),
        P(CTX, "head"),
        P(),
        P("head", None, None, None),
        P("head", None),
    )
    return jax.shard_map(
        shards, mesh=fine, in_specs=in_specs, out_specs=P(CTX, "head"), check_vma=False
    )
```

```python
import functools
import math

import jax
import jax.numpy as jnp
from jax import lax
from jax.experimental import pallas as pl
from jax.experimental.pallas import tpu as pltpu
from jax.sharding import Mesh, PartitionSpec as P


RING = 4
TILES = 4
CTX = ("z", "p")
VMEM = pl.BlockSpec(memory_space=pltpu.VMEM)
SMEM = pl.BlockSpec(memory_space=pltpu.SMEM)
LOWEST = -1e30
VMEM_BYTES = 24 << 20


def passed_along(value, steps):
    count = lax.axis_size(CTX)
    return lax.ppermute(value, CTX, [(source, source + steps) for source in range(count - steps)])


def resting(value):
    return pltpu.with_memory_space_constraint(value, pltpu.MemorySpace.HBM)


def product(left, right, left_dim, right_dim):
    return lax.dot_general(
        left,
        right,
        (((left_dim,), (right_dim,)), ((), ())),
        preferred_element_type=jnp.float32,
    )


def place_count(counts_ref, place_ref, back_step):
    place = place_ref[0] - back_step
    return jnp.where(place >= 0, counts_ref[jnp.maximum(place, 0)], 0)


def gradient_kernel(
    place_ref,
    counts_ref,
    rates_ref,
    keys_ref,
    values_ref,
    weights_ref,
    grad_ref,
    pairs_ref,
    held_keys,
    held_values,
    held_weights,
    held_grad,
    held_pairs,
    load_sems,
    store_sems,
):
    tokens, heads, width = held_keys.shape
    mats = held_weights.shape[1]

    def weight_load(head, index):
        return pltpu.make_async_copy(
            weights_ref.at[head, index],
            held_weights.at[head, index],
            load_sems.at[2 + head * mats + index],
        )

    keys_load = pltpu.make_async_copy(keys_ref, held_keys, load_sems.at[0])
    values_load = pltpu.make_async_copy(values_ref, held_values, load_sems.at[1])
    keys_load.start()
    weight_load(0, 0).start()
    weight_load(0, 1).start()
    values_load.start()
    weight_load(0, 2).start()
    for head in range(1, heads):
        for index in range(mats):
            weight_load(head, index).start()
    valid = lax.broadcasted_iota(jnp.int32, (tokens, 1), 0) < place_count(counts_ref, place_ref, 0)
    rates_all = jnp.concatenate(
        [rates_ref[...], jnp.zeros((8 - heads, tokens), jnp.float32)], 0
    ).T
    stores = []

    def store(source, target):
        stores.append(pltpu.make_async_copy(source, target, store_sems.at[len(stores)]))
        stores[-1].start()

    keys_load.wait()
    head_keys = []
    for head in range(heads):
        head_keys.append(held_keys[:, head, :])
        held_pairs[0, head] = head_keys[head]
        store(held_pairs.at[0, head], pairs_ref.at[0, head])
    for head in range(heads):
        keys = head_keys[head]
        weight_load(head, 0).wait()
        gate_pre = product(keys, held_weights[head, 0].astype(jnp.bfloat16), 1, 1)
        weight_load(head, 1).wait()
        up_pre = product(keys, held_weights[head, 1].astype(jnp.bfloat16), 1, 1)
        if head == 0:
            values_load.wait()
        values = held_values[:, head, :]
        held_pairs[1, head] = values
        store(held_pairs.at[1, head], pairs_ref.at[1, head])
        rates = jnp.where(valid, rates_all[:, head : head + 1], 0.0)
        scaled = (rates * values.astype(jnp.float32)).astype(jnp.bfloat16)
        weight_load(head, 2).wait()
        back = -product(scaled, held_weights[head, 2].astype(jnp.bfloat16), 1, 0)
        sigmoid = jax.nn.sigmoid(gate_pre)
        gate_act = gate_pre * sigmoid
        hidden = (gate_act * up_pre).astype(jnp.bfloat16)
        slope = sigmoid * (1.0 + gate_pre * (1.0 - sigmoid))
        grad_gate = (back * up_pre * slope).astype(jnp.bfloat16)
        grad_up = (back * gate_act).astype(jnp.bfloat16)
        factors = ((grad_gate, keys, 1.0), (grad_up, keys, 1.0), (scaled, hidden, -1.0))
        for index, (left, right, sign) in enumerate(factors):
            rows = pl.ds((head * mats + index) * width, width)
            held_grad[rows] = (sign * product(left, right, 0, 0)).astype(jnp.bfloat16)
            store(held_grad.at[rows], grad_ref.at[rows])
    for started in stores:
        started.wait()


def local_gradient(place, counts, token_keys, token_values, step_rates, fast_weights):
    heads, mats, width, _ = fast_weights.shape
    grad = jax.ShapeDtypeStruct((heads * mats * width, width), jnp.bfloat16)
    pairs = jax.ShapeDtypeStruct((2, heads, token_keys.shape[0], width), jnp.bfloat16)
    apart = pl.BlockSpec(memory_space=pl.ANY)
    return pl.pallas_call(
        gradient_kernel,
        out_shape=(grad, pairs),
        in_specs=[SMEM, SMEM, VMEM, apart, apart, apart],
        out_specs=(apart, apart),
        scratch_shapes=[
            pltpu.VMEM(token_keys.shape, jnp.bfloat16),
            pltpu.VMEM(token_values.shape, jnp.bfloat16),
            pltpu.VMEM(fast_weights.shape, jnp.float32),
            pltpu.VMEM(grad.shape, jnp.bfloat16),
            pltpu.VMEM(pairs.shape, jnp.bfloat16),
            pltpu.SemaphoreType.DMA((2 + heads * mats,)),
            pltpu.SemaphoreType.DMA(((2 + mats) * heads,)),
        ],
        name="gradient",
        cost_estimate=pl.CostEstimate(
            flops=14 * 256 * width * width * heads, transcendentals=131072, bytes_accessed=3000000
        ),
    )(place, counts, step_rates.T, token_keys, token_values, fast_weights)


def window_kernel(place_ref, counts_ref, queries_ref, own_ref, near_ref, far_ref, window_ref, turned_ref):
    tokens, heads, width = queries_ref.shape
    row = lax.broadcasted_iota(jnp.int32, (tokens, tokens), 0)
    column = lax.broadcasted_iota(jnp.int32, (tokens, tokens), 1)
    blocks = (
        (own_ref, (column <= row) & (column < place_count(counts_ref, place_ref, 0))),
        (near_ref, column < place_count(counts_ref, place_ref, 1)),
        (far_ref, (column > row) & (column < place_count(counts_ref, place_ref, 2))),
    )
    scale = 1.0 / math.sqrt(width)
    for head in range(heads):
        queries = queries_ref[:, head, :]
        turned_ref[head] = queries
        scores = [
            jnp.where(allowed, product(queries, block[0, head], 1, 1) * scale, LOWEST)
            for block, allowed in blocks
        ]
        top = jnp.max(functools.reduce(jnp.maximum, scores), axis=1, keepdims=True)
        expo = [jnp.exp(score - top) for score in scores]
        mass = jnp.sum(sum(expo), axis=1, keepdims=True)
        total = sum(
            product(part.astype(jnp.bfloat16), block[1, head], 1, 0)
            for part, (block, _) in zip(expo, blocks)
        )
        window_ref[:, head * width : (head + 1) * width] = total / mass


def window_attention(place, counts, queries, own, near, far):
    tokens, heads, width = queries.shape
    return pl.pallas_call(
        window_kernel,
        out_shape=(
            jax.ShapeDtypeStruct((tokens, heads * width), jnp.float32),
            jax.ShapeDtypeStruct((heads, tokens, width), jnp.bfloat16),
        ),
        in_specs=[SMEM, SMEM] + [VMEM] * 4,
        out_specs=(VMEM, VMEM),
        name="window",
        compiler_params=pltpu.CompilerParams(vmem_limit_bytes=VMEM_BYTES),
        cost_estimate=pl.CostEstimate(
            flops=12 * tokens * tokens * width * heads,
            transcendentals=400000,
            bytes_accessed=3000000,
        ),
    )(place, counts, queries, own, near, far)


def feature_kernel(
    place_ref,
    counts_ref,
    queries_ref,
    window_ref,
    weights_ref,
    own_weight_ref,
    features_ref,
    brought_ref,
    sem,
):
    brought = pltpu.make_async_copy(own_weight_ref, brought_ref, sem)
    brought.start()
    heads, tokens, width = queries_ref.shape
    valid = lax.broadcasted_iota(jnp.int32, (tokens, 1), 0) < place_count(counts_ref, place_ref, 0)
    for head in range(heads):
        queries = queries_ref[head]
        first = head * 3 * width
        gate = product(queries, weights_ref[first : first + width, :], 1, 1)
        up = product(queries, weights_ref[first + width : first + 2 * width, :], 1, 1)
        hidden = (gate * jax.nn.sigmoid(gate) * up).astype(jnp.bfloat16)
        learned = product(hidden, weights_ref[first + 2 * width : first + 3 * width, :], 1, 1)
        columns = slice(head * width, (head + 1) * width)
        features_ref[:, columns] = jnp.where(
            valid, learned + window_ref[:, columns], 0.0
        ).astype(jnp.bfloat16)
    brought.wait()


def features_of(place, counts, queries, window, new_flat, own_weight):
    heads, tokens, width = queries.shape
    return pl.pallas_call(
        feature_kernel,
        out_shape=(
            jax.ShapeDtypeStruct((tokens, heads * width), jnp.bfloat16),
            jax.ShapeDtypeStruct(own_weight.shape, jnp.bfloat16),
        ),
        in_specs=[SMEM, SMEM] + [VMEM] * 3 + [pl.BlockSpec(memory_space=pl.ANY)],
        out_specs=(VMEM, VMEM),
        scratch_shapes=[pltpu.SemaphoreType.DMA],
        name="features",
        compiler_params=pltpu.CompilerParams(vmem_limit_bytes=VMEM_BYTES),
        cost_estimate=pl.CostEstimate(
            flops=6 * tokens * width * width * heads, transcendentals=131072, bytes_accessed=2000000
        ),
    )(place, counts, queries, window, new_flat, own_weight)


def split_kernel(place_ref, mine_in_ref, theirs_in_ref, mine_ref, theirs_ref):
    mine_ref[0] = mine_in_ref[...]
    theirs_ref[0] = theirs_in_ref[...]


def column_halves(head_place, out_weight):
    depth, columns = out_weight.shape
    tile = columns // 2 // TILES
    piece = jax.ShapeDtypeStruct((TILES, depth, tile), out_weight.dtype)
    out_spec = pl.BlockSpec((1, depth, tile), lambda step, place: (step, 0, 0))
    return pl.pallas_call(
        split_kernel,
        out_shape=(piece, piece),
        grid_spec=pltpu.PrefetchScalarGridSpec(
            num_scalar_prefetch=1,
            grid=(TILES,),
            in_specs=[
                pl.BlockSpec((depth, tile), lambda step, place: (0, place[0] * TILES + step)),
                pl.BlockSpec((depth, tile), lambda step, place: (0, (1 - place[0]) * TILES + step)),
            ],
            out_specs=(out_spec, out_spec),
        ),
        name="split",
        cost_estimate=pl.CostEstimate(flops=0, transcendentals=0, bytes_accessed=8000000),
    )(head_place, out_weight, out_weight)


def own_project_kernel(own_ref, weight_ref, theirs_ref, out_ref, brought_ref, sem):
    brought = pltpu.make_async_copy(theirs_ref, brought_ref, sem)
    brought.start()
    tile = weight_ref.shape[2]
    for step in range(TILES):
        out_ref[:, step * tile : (step + 1) * tile] = jnp.dot(
            own_ref[...], weight_ref[step], preferred_element_type=jnp.float32
        )
    brought.wait()


def own_projected(own, weight, theirs):
    return pl.pallas_call(
        own_project_kernel,
        out_shape=(
            jax.ShapeDtypeStruct((own.shape[0], TILES * weight.shape[2]), jnp.float32),
            jax.ShapeDtypeStruct(theirs.shape, jnp.bfloat16),
        ),
        in_specs=[VMEM, VMEM, pl.BlockSpec(memory_space=pl.ANY)],
        out_specs=(VMEM, VMEM),
        scratch_shapes=[pltpu.SemaphoreType.DMA],
        name="own_project",
        compiler_params=pltpu.CompilerParams(vmem_limit_bytes=VMEM_BYTES),
        cost_estimate=pl.CostEstimate(
            flops=2 * own.shape[0] * theirs.size, transcendentals=0, bytes_accessed=4000000
        ),
    )(own, weight, theirs)


def project_kernel(other_ref, weight_ref, own_ref, out_ref, held_out, sems):
    tile = held_out.shape[2]
    stores = []
    for step in range(TILES):
        columns = slice(step * tile, (step + 1) * tile)
        held_out[step] = (
            own_ref[:, columns]
            + jnp.dot(other_ref[...], weight_ref[step], preferred_element_type=jnp.float32)
        ).astype(jnp.bfloat16)
        stores.append(
            pltpu.make_async_copy(held_out.at[step], out_ref.at[:, columns], sems.at[step])
        )
        stores[step].start()
    for store in stores:
        store.wait()


def projected(other, weight, own_product):
    tokens = other.shape[0]
    tile = weight.shape[2]
    return pl.pallas_call(
        project_kernel,
        out_shape=jax.ShapeDtypeStruct((tokens, TILES * tile), jnp.bfloat16),
        in_specs=[VMEM, VMEM, VMEM],
        out_specs=pl.BlockSpec(memory_space=pl.ANY),
        scratch_shapes=[
            pltpu.VMEM((TILES, tokens, tile), jnp.bfloat16),
            pltpu.SemaphoreType.DMA((TILES,)),
        ],
        name="project",
        compiler_params=pltpu.CompilerParams(vmem_limit_bytes=VMEM_BYTES),
        cost_estimate=pl.CostEstimate(
            flops=2 * tokens * weight.size, transcendentals=0, bytes_accessed=6000000
        ),
    )(other, weight, own_product)


def collect_kernel(blocks_ref, sums_ref):
    total = jnp.sum(blocks_ref[...].astype(jnp.float32), axis=0)
    sums_ref[...] = jnp.broadcast_to(total[None], sums_ref.shape)


def collected(copies, blocks):
    return pl.pallas_call(
        collect_kernel,
        out_shape=jax.ShapeDtypeStruct((copies, *blocks.shape[1:]), jnp.float32),
        in_specs=[VMEM],
        out_specs=VMEM,
        name="collect",
        compiler_params=pltpu.CompilerParams(vmem_limit_bytes=VMEM_BYTES),
        cost_estimate=pl.CostEstimate(flops=400000, transcendentals=0, bytes_accessed=800000),
    )(blocks)


def refresh_kernel(total, sums_ref, old_ref, rows_ref):
    gradient = jnp.sum(sums_ref[...], axis=0)
    old = old_ref[...]
    updated = old - gradient / math.sqrt(total)
    old_norm = jnp.sqrt(jnp.sum(old * old, axis=1, keepdims=True))
    fresh = updated * old_norm / jnp.sqrt(jnp.sum(updated * updated, axis=1, keepdims=True) + 1e-06)
    rows_ref[...] = jnp.broadcast_to(fresh.astype(jnp.bfloat16)[None], rows_ref.shape)


def refreshed(total, copies, sums, old_rows):
    return pl.pallas_call(
        functools.partial(refresh_kernel, total),
        out_shape=jax.ShapeDtypeStruct((copies, *old_rows.shape), jnp.bfloat16),
        in_specs=[VMEM, VMEM],
        out_specs=VMEM,
        name="refresh",
        compiler_params=pltpu.CompilerParams(vmem_limit_bytes=VMEM_BYTES),
        cost_estimate=pl.CostEstimate(flops=100000, transcendentals=0, bytes_accessed=1000000),
    )(sums, old_rows)


def shards(queries, token_keys, token_values, step_rates, counts, fast_weights, out_weight):
    tok_rows, _, head_width = queries.shape
    device_count, plane_count = lax.axis_size(CTX), lax.axis_size("p")
    plane_place, head_place = lax.axis_index("p"), lax.axis_index("head")
    place = lax.axis_index(CTX).reshape(1).astype(jnp.int32)
    local_grad, pairs = local_gradient(
        place, counts, token_keys, token_values, step_rates, fast_weights
    )
    near = passed_along(pairs, 1)
    blocks = lax.all_to_all(local_grad.reshape(plane_count, -1, head_width), "p", 0, 0, tiled=True)
    out_own, out_theirs = column_halves(
        head_place.reshape(1).astype(jnp.int32), out_weight
    )
    out_other = lax.ppermute(out_theirs, "head", [(0, 1), (1, 0)])
    sums = collected(RING, blocks)
    sums = lax.all_to_all(sums, "z", 0, 0, tiled=True)
    far = passed_along(near, 1)
    old_flat = fast_weights.reshape(-1, head_width)
    own_rows = old_flat.shape[0] // plane_count
    old_rows = lax.dynamic_slice_in_dim(old_flat, plane_place * own_rows, own_rows, 0)
    new_rows = refreshed(tok_rows * device_count, plane_count, sums, old_rows)
    new_flat = lax.all_to_all(new_rows, "p", 0, 0, tiled=True).reshape(-1, head_width)
    window, turned_queries = window_attention(place, counts, queries, pairs, near, far)
    features, own_weight = features_of(
        place, counts, turned_queries, window, new_flat, resting(out_own)
    )
    other = lax.ppermute(features, "head", [(0, 1), (1, 0)])
    own_product, brought = own_projected(features, own_weight, resting(out_other))
    return projected(other, brought, own_product)


def solution(mesh):
    fine = Mesh(mesh.devices.reshape(RING, -1, 2), ("z", "p", "head"))
    in_specs = (
        P(CTX, "head", None),
        P(CTX, "head", None),
        P(CTX, "head", None),
        P(CTX, "head"),
        P(),
        P("head", None, None, None),
        P("head", None),
    )
    return jax.shard_map(
        shards, mesh=fine, in_specs=in_specs, out_specs=P(CTX, "head"), check_vma=False
    )
```

```python
import functools
import math

import jax
import jax.numpy as jnp
from jax import lax
from jax.experimental import pallas as pl
from jax.experimental.pallas import tpu as pltpu
from jax.sharding import Mesh, PartitionSpec as P


RING = 4
TILES = 4
CTX = ("z", "p")
VMEM = pl.BlockSpec(memory_space=pltpu.VMEM)
SMEM = pl.BlockSpec(memory_space=pltpu.SMEM)
LOWEST = -1e30
VMEM_BYTES = 24 << 20


def passed_along(value, steps):
    count = lax.axis_size(CTX)
    return lax.ppermute(value, CTX, [(source, source + steps) for source in range(count - steps)])


def resting(value):
    return pltpu.with_memory_space_constraint(value, pltpu.MemorySpace.HBM)


def product(left, right, left_dim, right_dim):
    return lax.dot_general(
        left,
        right,
        (((left_dim,), (right_dim,)), ((), ())),
        preferred_element_type=jnp.float32,
    )


def place_count(counts_ref, place_ref, back_step):
    place = place_ref[0] - back_step
    return jnp.where(place >= 0, counts_ref[jnp.maximum(place, 0)], 0)


def gradient_kernel(
    place_ref, counts_ref, keys_ref, values_ref, rates_ref, weights_ref, grad_ref, pairs_ref
):
    tokens, heads, width = keys_ref.shape

    def one_head(head):
        valid = lax.broadcasted_iota(jnp.int32, (tokens, 1), 0) < place_count(
            counts_ref, place_ref, 0
        )
        rates_all = jnp.concatenate(
            [rates_ref[...], jnp.zeros((8 - heads, tokens), jnp.float32)], 0
        ).T
        keys, values = keys_ref[:, head, :], values_ref[:, head, :]
        pairs_ref[0, 0] = keys
        pairs_ref[1, 0] = values
        rates = jnp.where(valid, rates_all[:, head : head + 1], 0.0)
        scaled = (rates * values.astype(jnp.float32)).astype(jnp.bfloat16)
        gate_weight = weights_ref[0, 0].astype(jnp.bfloat16)
        up_weight = weights_ref[0, 1].astype(jnp.bfloat16)
        down_weight = weights_ref[0, 2].astype(jnp.bfloat16)
        gate_pre = product(keys, gate_weight, 1, 1)
        up_pre = product(keys, up_weight, 1, 1)
        back = -product(scaled, down_weight, 1, 0)
        sigmoid = jax.nn.sigmoid(gate_pre)
        gate_act = gate_pre * sigmoid
        hidden = (gate_act * up_pre).astype(jnp.bfloat16)
        slope = sigmoid * (1.0 + gate_pre * (1.0 - sigmoid))
        grad_gate = (back * up_pre * slope).astype(jnp.bfloat16)
        grad_up = (back * gate_act).astype(jnp.bfloat16)
        mats = (
            product(grad_gate, keys, 0, 0),
            product(grad_up, keys, 0, 0),
            -product(scaled, hidden, 0, 0),
        )
        for index, mat in enumerate(mats):
            grad_ref[index * width : (index + 1) * width, :] = mat.astype(jnp.bfloat16)

    for head in range(heads):
        pl.when(pl.program_id(0) == head)(functools.partial(one_head, head))


def local_gradient(place, counts, token_keys, token_values, step_rates, fast_weights):
    heads, mats, width, _ = fast_weights.shape
    tokens = token_keys.shape[0]
    raw = pl.BlockSpec((tokens, heads, width), lambda head: (0, 0, 0))
    return pl.pallas_call(
        gradient_kernel,
        out_shape=(
            jax.ShapeDtypeStruct((heads * mats * width, width), jnp.bfloat16),
            jax.ShapeDtypeStruct((2, heads, tokens, width), jnp.bfloat16),
        ),
        grid=(heads,),
        in_specs=[
            SMEM,
            SMEM,
            raw,
            raw,
            pl.BlockSpec((heads, tokens), lambda head: (0, 0)),
            pl.BlockSpec((1, mats, width, width), lambda head: (head, 0, 0, 0)),
        ],
        out_specs=(
            pl.BlockSpec((mats * width, width), lambda head: (head, 0)),
            pl.BlockSpec((2, 1, tokens, width), lambda head: (0, head, 0, 0)),
        ),
        name="gradient",
        cost_estimate=pl.CostEstimate(
            flops=14 * 256 * width * width * heads, transcendentals=131072, bytes_accessed=3000000
        ),
    )(place, counts, token_keys, token_values, step_rates.T, fast_weights)


def window_kernel(place_ref, counts_ref, queries_ref, own_ref, near_ref, far_ref, window_ref, turned_ref):
    tokens, heads, width = queries_ref.shape
    row = lax.broadcasted_iota(jnp.int32, (tokens, tokens), 0)
    column = lax.broadcasted_iota(jnp.int32, (tokens, tokens), 1)
    blocks = (
        (own_ref, (column <= row) & (column < place_count(counts_ref, place_ref, 0))),
        (near_ref, column < place_count(counts_ref, place_ref, 1)),
        (far_ref, (column > row) & (column < place_count(counts_ref, place_ref, 2))),
    )
    scale = 1.0 / math.sqrt(width)
    for head in range(heads):
        queries = queries_ref[:, head, :]
        turned_ref[head] = queries
        scores = [
            jnp.where(allowed, product(queries, block[0, head], 1, 1) * scale, LOWEST)
            for block, allowed in blocks
        ]
        top = jnp.max(functools.reduce(jnp.maximum, scores), axis=1, keepdims=True)
        expo = [jnp.exp(score - top) for score in scores]
        mass = jnp.sum(sum(expo), axis=1, keepdims=True)
        total = sum(
            product(part.astype(jnp.bfloat16), block[1, head], 1, 0)
            for part, (block, _) in zip(expo, blocks)
        )
        window_ref[:, head * width : (head + 1) * width] = total / mass


def window_attention(place, counts, queries, own, near, far):
    tokens, heads, width = queries.shape
    return pl.pallas_call(
        window_kernel,
        out_shape=(
            jax.ShapeDtypeStruct((tokens, heads * width), jnp.float32),
            jax.ShapeDtypeStruct((heads, tokens, width), jnp.bfloat16),
        ),
        in_specs=[SMEM, SMEM] + [VMEM] * 4,
        out_specs=(VMEM, VMEM),
        name="window",
        compiler_params=pltpu.CompilerParams(vmem_limit_bytes=VMEM_BYTES),
        cost_estimate=pl.CostEstimate(
            flops=12 * tokens * tokens * width * heads,
            transcendentals=400000,
            bytes_accessed=3000000,
        ),
    )(place, counts, queries, own, near, far)


def feature_kernel(
    place_ref,
    counts_ref,
    queries_ref,
    window_ref,
    weights_ref,
    own_weight_ref,
    features_ref,
    brought_ref,
    sem,
):
    brought = pltpu.make_async_copy(own_weight_ref, brought_ref, sem)
    brought.start()
    heads, tokens, width = queries_ref.shape
    valid = lax.broadcasted_iota(jnp.int32, (tokens, 1), 0) < place_count(counts_ref, place_ref, 0)
    for head in range(heads):
        queries = queries_ref[head]
        first = head * 3 * width
        gate = product(queries, weights_ref[first : first + width, :], 1, 1)
        up = product(queries, weights_ref[first + width : first + 2 * width, :], 1, 1)
        hidden = (gate * jax.nn.sigmoid(gate) * up).astype(jnp.bfloat16)
        learned = product(hidden, weights_ref[first + 2 * width : first + 3 * width, :], 1, 1)
        columns = slice(head * width, (head + 1) * width)
        features_ref[:, columns] = jnp.where(
            valid, learned + window_ref[:, columns], 0.0
        ).astype(jnp.bfloat16)
    brought.wait()


def features_of(place, counts, queries, window, new_flat, own_weight):
    heads, tokens, width = queries.shape
    return pl.pallas_call(
        feature_kernel,
        out_shape=(
            jax.ShapeDtypeStruct((tokens, heads * width), jnp.bfloat16),
            jax.ShapeDtypeStruct(own_weight.shape, jnp.bfloat16),
        ),
        in_specs=[SMEM, SMEM] + [VMEM] * 3 + [pl.BlockSpec(memory_space=pl.ANY)],
        out_specs=(VMEM, VMEM),
        scratch_shapes=[pltpu.SemaphoreType.DMA],
        name="features",
        compiler_params=pltpu.CompilerParams(vmem_limit_bytes=VMEM_BYTES),
        cost_estimate=pl.CostEstimate(
            flops=6 * tokens * width * width * heads, transcendentals=131072, bytes_accessed=2000000
        ),
    )(place, counts, queries, window, new_flat, own_weight)


def split_kernel(place_ref, mine_in_ref, theirs_in_ref, mine_ref, theirs_ref):
    mine_ref[0] = mine_in_ref[...]
    theirs_ref[0] = theirs_in_ref[...]


def column_halves(head_place, out_weight):
    depth, columns = out_weight.shape
    tile = columns // 2 // TILES
    piece = jax.ShapeDtypeStruct((TILES, depth, tile), out_weight.dtype)
    out_spec = pl.BlockSpec((1, depth, tile), lambda step, place: (step, 0, 0))
    return pl.pallas_call(
        split_kernel,
        out_shape=(piece, piece),
        grid_spec=pltpu.PrefetchScalarGridSpec(
            num_scalar_prefetch=1,
            grid=(TILES,),
            in_specs=[
                pl.BlockSpec((depth, tile), lambda step, place: (0, place[0] * TILES + step)),
                pl.BlockSpec((depth, tile), lambda step, place: (0, (1 - place[0]) * TILES + step)),
            ],
            out_specs=(out_spec, out_spec),
        ),
        name="split",
        cost_estimate=pl.CostEstimate(flops=0, transcendentals=0, bytes_accessed=8000000),
    )(head_place, out_weight, out_weight)


def own_project_kernel(own_ref, weight_ref, theirs_ref, out_ref, brought_ref, sem):
    brought = pltpu.make_async_copy(theirs_ref, brought_ref, sem)
    brought.start()
    tile = weight_ref.shape[2]
    for step in range(TILES):
        out_ref[:, step * tile : (step + 1) * tile] = jnp.dot(
            own_ref[...], weight_ref[step], preferred_element_type=jnp.float32
        )
    brought.wait()


def own_projected(own, weight, theirs):
    return pl.pallas_call(
        own_project_kernel,
        out_shape=(
            jax.ShapeDtypeStruct((own.shape[0], TILES * weight.shape[2]), jnp.float32),
            jax.ShapeDtypeStruct(theirs.shape, jnp.bfloat16),
        ),
        in_specs=[VMEM, VMEM, pl.BlockSpec(memory_space=pl.ANY)],
        out_specs=(VMEM, VMEM),
        scratch_shapes=[pltpu.SemaphoreType.DMA],
        name="own_project",
        compiler_params=pltpu.CompilerParams(vmem_limit_bytes=VMEM_BYTES),
        cost_estimate=pl.CostEstimate(
            flops=2 * own.shape[0] * theirs.size, transcendentals=0, bytes_accessed=4000000
        ),
    )(own, weight, theirs)


def project_kernel(other_ref, weight_ref, own_ref, out_ref, held_out, sems):
    tile = held_out.shape[2]
    stores = []
    for step in range(TILES):
        columns = slice(step * tile, (step + 1) * tile)
        held_out[step] = (
            own_ref[:, columns]
            + jnp.dot(other_ref[...], weight_ref[step], preferred_element_type=jnp.float32)
        ).astype(jnp.bfloat16)
        stores.append(
            pltpu.make_async_copy(held_out.at[step], out_ref.at[:, columns], sems.at[step])
        )
        stores[step].start()
    for store in stores:
        store.wait()


def projected(other, weight, own_product):
    tokens = other.shape[0]
    tile = weight.shape[2]
    return pl.pallas_call(
        project_kernel,
        out_shape=jax.ShapeDtypeStruct((tokens, TILES * tile), jnp.bfloat16),
        in_specs=[VMEM, VMEM, VMEM],
        out_specs=pl.BlockSpec(memory_space=pl.ANY),
        scratch_shapes=[
            pltpu.VMEM((TILES, tokens, tile), jnp.bfloat16),
            pltpu.SemaphoreType.DMA((TILES,)),
        ],
        name="project",
        compiler_params=pltpu.CompilerParams(vmem_limit_bytes=VMEM_BYTES),
        cost_estimate=pl.CostEstimate(
            flops=2 * tokens * weight.size, transcendentals=0, bytes_accessed=6000000
        ),
    )(other, weight, own_product)


def collect_kernel(blocks_ref, sums_ref):
    total = jnp.sum(blocks_ref[...].astype(jnp.float32), axis=0)
    sums_ref[...] = jnp.broadcast_to(total[None], sums_ref.shape)


def collected(copies, blocks):
    return pl.pallas_call(
        collect_kernel,
        out_shape=jax.ShapeDtypeStruct((copies, *blocks.shape[1:]), jnp.float32),
        in_specs=[VMEM],
        out_specs=VMEM,
        name="collect",
        compiler_params=pltpu.CompilerParams(vmem_limit_bytes=VMEM_BYTES),
        cost_estimate=pl.CostEstimate(flops=400000, transcendentals=0, bytes_accessed=800000),
    )(blocks)


def refresh_kernel(total, sums_ref, old_ref, rows_ref):
    gradient = jnp.sum(sums_ref[...], axis=0)
    old = old_ref[...]
    updated = old - gradient / math.sqrt(total)
    old_norm = jnp.sqrt(jnp.sum(old * old, axis=1, keepdims=True))
    fresh = updated * old_norm / jnp.sqrt(jnp.sum(updated * updated, axis=1, keepdims=True) + 1e-06)
    rows_ref[...] = jnp.broadcast_to(fresh.astype(jnp.bfloat16)[None], rows_ref.shape)


def refreshed(total, copies, sums, old_rows):
    return pl.pallas_call(
        functools.partial(refresh_kernel, total),
        out_shape=jax.ShapeDtypeStruct((copies, *old_rows.shape), jnp.bfloat16),
        in_specs=[VMEM, VMEM],
        out_specs=VMEM,
        name="refresh",
        compiler_params=pltpu.CompilerParams(vmem_limit_bytes=VMEM_BYTES),
        cost_estimate=pl.CostEstimate(flops=100000, transcendentals=0, bytes_accessed=1000000),
    )(sums, old_rows)


def shards(queries, token_keys, token_values, step_rates, counts, fast_weights, out_weight):
    tok_rows, _, head_width = queries.shape
    device_count, plane_count = lax.axis_size(CTX), lax.axis_size("p")
    plane_place, head_place = lax.axis_index("p"), lax.axis_index("head")
    place = lax.axis_index(CTX).reshape(1).astype(jnp.int32)
    local_grad, pairs = local_gradient(
        place, counts, token_keys, token_values, step_rates, fast_weights
    )
    near = passed_along(pairs, 1)
    blocks = lax.all_to_all(local_grad.reshape(plane_count, -1, head_width), "p", 0, 0, tiled=True)
    out_own, out_theirs = column_halves(
        head_place.reshape(1).astype(jnp.int32), out_weight
    )
    out_other = lax.ppermute(out_theirs, "head", [(0, 1), (1, 0)])
    sums = collected(RING, blocks)
    sums = lax.all_to_all(sums, "z", 0, 0, tiled=True)
    far = passed_along(near, 1)
    old_flat = fast_weights.reshape(-1, head_width)
    own_rows = old_flat.shape[0] // plane_count
    old_rows = lax.dynamic_slice_in_dim(old_flat, plane_place * own_rows, own_rows, 0)
    new_rows = refreshed(tok_rows * device_count, plane_count, sums, old_rows)
    new_flat = lax.all_to_all(new_rows, "p", 0, 0, tiled=True).reshape(-1, head_width)
    window, turned_queries = window_attention(place, counts, queries, pairs, near, far)
    features, own_weight = features_of(
        place, counts, turned_queries, window, new_flat, resting(out_own)
    )
    other = lax.ppermute(features, "head", [(0, 1), (1, 0)])
    own_product, brought = own_projected(features, own_weight, resting(out_other))
    return projected(other, brought, own_product)


def solution(mesh):
    fine = Mesh(mesh.devices.reshape(RING, -1, 2), ("z", "p", "head"))
    in_specs = (
        P(CTX, "head", None),
        P(CTX, "head", None),
        P(CTX, "head", None),
        P(CTX, "head"),
        P(),
        P("head", None, None, None),
        P("head", None),
    )
    return jax.shard_map(
        shards, mesh=fine, in_specs=in_specs, out_specs=P(CTX, "head"), check_vma=False
    )
```
